768 devices in a mesh: grp: 48 (over y, z_lo), gy: 4 (over z_hi, core), gz: 4 (over x).
Axes of the slice: x: 4, y: 8, z: 12 (z_hi: 2, z_lo: 6; z = z_hi * 6 + z_lo), core: 2. Of those that a mesh axis runs over, the one named last changes fastest.
Arguments:
- fwd_velocity: float32 [3, 192, 32, 512], P(None, 'grp', 'gy', 'gz'), may hold values from -6 to 6
- fwd_stress: float32 [6, 192, 32, 512], P(None, 'grp', 'gy', 'gz'), may hold values from -6 to 6
- density: float32 [192, 32, 512], P('grp', 'gy', 'gz'), may hold values from 1 to 3
- lame: float32 [2, 192, 32, 512], P(None, 'grp', 'gy', 'gz'), may hold values from 0.5 to 2
- adj_velocity: float32 [3, 288, 32, 512], P(None, 'grp', 'gy', 'gz'), may hold values from -6 to 6
- adj_stress: float32 [6, 288, 32, 512], P(None, 'grp', 'gy', 'gz'), may hold values from -6 to 6
- offsets: int32 [48], replicated, may hold values from 0 to 2, as said below
Outputs:
- density_kernel: float32 [288, 32, 512], P('grp', 'gy', 'gz')
- modulus_kernel: float32 [2, 288, 32, 512], P(None, 'grp', 'gy', 'gz')
The draws below stay inside these ranges and needn't reach their ends.
Inputs may be any that keep to these rules, and one draw needn't show every extreme that they name: offsets[0] is 0; in every draw some block b has offsets[b] = 0 and offsets[b+1] = 2, so some adjoint block has 6 planes.
All inputs are finite; a program needn't handle non-finite values.
Results may differ from the reference program's by a relative error of at most 0.00002.
Values sent between devices are 32-bit elements; how exact they have to be, the bound alone decides.
No kernel may reach another device: no remote copies, remote signals or barrier semaphores. Data moves between devices by JAX's collectives and lax.ppermute only.
A program may use at most 32 MiB of HBM per device.

```python
import math
import jax
import jax.numpy as jnp

CX = 4
STEPS = 4
LAG = 2
CAP = 6
NBLK = 48
NX = 192
NY = 32
NZ = 512
NXA = 288


def draw_offsets(key, part):
    seeded = jax.random.fold_in(key, 17)
    first, second = jax.random.split(seeded)
    values = jax.random.randint(first, (NBLK,), 0, LAG + 1)
    chosen = jax.random.randint(second, (), 0, NBLK - 1)
    places = jnp.arange(NBLK)
    values = jnp.where(places == chosen, 0, values)
    values = jnp.where(places == chosen + 1, LAG, values)
    values = jnp.where(places == 0, 0, values)
    return values.astype(jnp.int32)


def shard_levels(rng, shape, shards, smallest, high):
    gain = 1.0
    for dim, parts in shards:
        heights = jax.random.uniform(jax.random.fold_in(jax.random.fold_in(rng, 6), dim), (parts,), jnp.float32, smallest / len(shards), high / len(shards))
        gain = gain * jnp.repeat(jnp.exp(heights), shape[dim] // parts).reshape((-1,) + (1,) * (len(shape) - 1 - dim))
    return gain


def scatter_about(own_key, extent, scale, reach, shards=(), held_as=jnp.bfloat16):
    drawn = jax.random.normal(own_key, extent, jnp.float32) * scale
    if len(shards) > 0:
        drawn = shard_levels(own_key, extent, shards, -0.22, 0.18) * drawn
    return jnp.clip(drawn, min=-reach, max=reach).astype(held_as)


def setup_inputs(seed: int = 0) -> dict:
    keys = jax.random.split(jax.random.key(seed), 8)
    fwd_velocity = scatter_about(keys[0], (3, NX, NY, NZ), 1.0, 6.0, ((1, 48), (2, 4), (3, 4)), jnp.float32)
    fwd_stress = scatter_about(keys[1], (6, NX, NY, NZ), 1.0, 6.0, ((1, 48), (2, 4), (3, 4)), jnp.float32)
    density = jnp.clip(1.0 + 2.0 * jax.random.uniform(keys[2], (NX, NY, NZ), jnp.float32) ** shard_levels(keys[2], (NX, NY, NZ), ((0, 48), (1, 4), (2, 4)), -0.2, 0.2), 1.0, 3.0)
    lame = jnp.clip(jnp.exp(math.log(2.0) - 1.3862944 * jax.random.uniform(keys[3], (2, NX, NY, NZ), jnp.float32) ** shard_levels(keys[3], (2, NX, NY, NZ), ((1, 48), (2, 4), (3, 4)), -0.2, 0.2)), 0.5, 2.0)
    adj_velocity = scatter_about(keys[4], (3, NXA, NY, NZ), 1.0, 6.0, ((1, 48), (2, 4), (3, 4)), jnp.float32)
    adj_stress = scatter_about(keys[5], (6, NXA, NY, NZ), 1.0, 6.0, ((1, 48), (2, 4), (3, 4)), jnp.float32)
    offsets = draw_offsets(jax.random.fold_in(keys[7], 71), 0)
    return {"fwd_velocity": fwd_velocity, "fwd_stress": fwd_stress, "density": density, "lame": lame, "adj_velocity": adj_velocity, "adj_stress": adj_stress, "offsets": offsets}


time_step = 0.15
pairs = ((0, 5, 4), (5, 1, 3), (4, 3, 2))


def global_diffs(stack):
    padded = jnp.pad(stack, ((0, 0), (1, 1), (1, 1), (1, 1)))
    along_x = (padded[:, 2:, 1:-1, 1:-1] - padded[:, :-2, 1:-1, 1:-1]) * 0.5
    along_y = (padded[:, 1:-1, 2:, 1:-1] - padded[:, 1:-1, :-2, 1:-1]) * 0.5
    along_z = (padded[:, 1:-1, 1:-1, 2:] - padded[:, 1:-1, 1:-1, :-2]) * 0.5
    return (along_x, along_y, along_z)


def velocity_update(velocity, stress, rho_field, delta, differ):
    slopes = differ(stress)
    result = []
    for i in range(3):
        force = slopes[0][pairs[i][0]] + slopes[1][pairs[i][1]] + slopes[2][pairs[i][2]]
        result.append(velocity[i] + (delta / rho_field) * force)
    return jnp.stack(result)


def strain_from(slopes, base):
    grads = [[slopes[j][base + i] for j in range(3)] for i in range(3)]
    return jnp.stack([grads[0][0], grads[1][1], grads[2][2],
                      0.5 * (grads[1][2] + grads[2][1]),
                      0.5 * (grads[0][2] + grads[2][0]),
                      0.5 * (grads[0][1] + grads[1][0])])


def stress_update(stress, strain, moduli, delta):
    trace = strain[0] + strain[1] + strain[2]
    first = moduli[0] * trace
    double = 2.0 * moduli[1]
    normal = stress[:3] + delta * (first[None] + double[None] * strain[:3])
    shear = stress[3:] + delta * (double[None] * strain[3:])
    return jnp.concatenate([normal, shear])


def kernel_terms(back_vel, fore_vel, back_rate, fore_rate):
    rho_term = time_step * (back_vel[0] * fore_vel[0] + back_vel[1] * fore_vel[1] + back_vel[2] * fore_vel[2])
    lam_term = time_step * ((back_rate[0] + back_rate[1] + back_rate[2]) * (fore_rate[0] + fore_rate[1] + fore_rate[2]))
    normal = back_rate[0] * fore_rate[0] + back_rate[1] * fore_rate[1] + back_rate[2] * fore_rate[2]
    shear = back_rate[3] * fore_rate[3] + back_rate[4] * fore_rate[4] + back_rate[5] * fore_rate[5]
    mu_term = time_step * (2.0 * (normal + 2.0 * shear))
    return rho_term, jnp.stack([lam_term, mu_term])


def reference(fwd_velocity, fwd_stress, density, lame, adj_velocity, adj_stress, offsets):
    blocks = jnp.arange(NBLK, dtype=jnp.int32)
    starts = blocks * CX + offsets
    following = jnp.concatenate([offsets[1:], jnp.zeros((1,), jnp.int32)])
    extents = CX + following - offsets
    planes = jnp.arange(NX, dtype=jnp.int32)
    owner = jnp.sum((planes[:, None] >= starts[None, 1:]).astype(jnp.int32), axis=1).astype(jnp.int32)
    where_held = (owner * CAP + planes - starts[owner]).astype(jnp.int32)
    slots = jnp.arange(NBLK * CAP, dtype=jnp.int32)
    slot_block = slots // CAP
    slot_row = slots % CAP
    live = slot_row < extents[slot_block]
    source = jnp.minimum(starts[slot_block] + slot_row, NX - 1).astype(jnp.int32)

    back_vel = jnp.take(adj_velocity, where_held, axis=1)
    back_str = jnp.take(adj_stress, where_held, axis=1)
    fore_vel = fwd_velocity
    fore_str = fwd_stress
    rho_kernel = jnp.zeros((NX, NY, NZ), jnp.float32)
    mod_kernel = jnp.zeros((2, NX, NY, NZ), jnp.float32)
    for step in range(STEPS):
        fore_vel = velocity_update(fore_vel, fore_str, density, -time_step, global_diffs)
        fore_rate = strain_from(global_diffs(fore_vel), 0)
        fore_str = stress_update(fore_str, fore_rate, lame, -time_step)
        back_vel = velocity_update(back_vel, back_str, density, time_step, global_diffs)
        back_rate = strain_from(global_diffs(back_vel), 0)
        back_str = stress_update(back_str, back_rate, lame, time_step)
        rho_term, mod_term = kernel_terms(back_vel, fore_vel, back_rate, fore_rate)
        rho_kernel = rho_kernel + rho_term
        mod_kernel = mod_kernel + mod_term
    live_rows = live[:, None, None]
    density_kernel = jnp.where(live_rows, jnp.take(rho_kernel, source, axis=0), jnp.float32(0.0))
    modulus_kernel = jnp.where(live_rows[None], jnp.take(mod_kernel, source, axis=1), jnp.float32(0.0))
    return density_kernel, modulus_kernel
```

```python
import functools

import jax
import jax.numpy as jnp
from jax import lax
from jax.experimental import pallas as pl
from jax.experimental.pallas import tpu as pltpu
from jax.sharding import PartitionSpec as P

STEPS = 4
H = 0.15
PAIRS = ((0, 5, 4), (5, 1, 3), (4, 3, 2))

VB, CB, LB, MB = 120, 168, 176, 182
N = 192
PA, PV, PS, PR, PL, NP1 = 0, 36, 45, 69, 72, 76
NF = 81


def swaps(count, first):
    out = []
    for i in range(first, count - 1, 2):
        out += [(i, i + 1), (i + 1, i)]
    return out


def both_swaps(value_a, value_b, axis):
    count = lax.axis_size(axis)
    second = lax.ppermute(value_b, axis, swaps(count, 1))
    first = lax.ppermute(value_a, axis, swaps(count, 0))
    return first, second


def pack_kernel(sc, fv, fs, rho, lam, av, as_, out_a, out_b):
    odd, off = sc[0], sc[1]
    for out, up in ((out_a, 1 - odd), (out_b, odd)):
        for i in range(4):
            row = jnp.maximum(2 * up + i - off, 0)
            for c in range(3):
                out[PA + i * 9 + c] = av[c, row]
            for c in range(6):
                out[PA + i * 9 + 3 + c] = as_[c, row]
                out[PS + i * 6 + c] = fs[c, i]
        for i in range(3):
            for c in range(3):
                out[PV + i * 3 + c] = fv[c, i + up]
            out[PR + i] = rho[i + up]
        for i in range(2):
            for c in range(2):
                out[PL + i * 2 + c] = lam[c, i]


def window_kernel(sc, fv, fs, rho, lam, av, as_, ra, rb, w):
    odd, off, noff = sc[0], sc[1], sc[2]
    low_is_a = odd == 1

    def low(n):
        return jnp.where(low_is_a, ra[n], rb[n])

    def high(n):
        return jnp.where(low_is_a, rb[n], ra[n])

    def adjoint(p, ref, c, slot):
        if p < 2:
            return low(PA + p * 9 + slot)
        if p > 7:
            return high(PA + (p - 6) * 9 + slot)
        j = p - 2
        own = ref[c, jnp.clip(j - off, 0, 5)]
        if j < 2:
            return jnp.where(j < off, low(PA + p * 9 + slot), own)
        if j > 3:
            return jnp.where(j - 4 < noff, own, high(PA + (p - 6) * 9 + slot))
        return own

    for p in range(10):
        for c in range(6):
            if p < 2:
                f = low(PS + (p + 2) * 6 + c)
            elif p < 6:
                f = fs[c, p - 2]
            else:
                f = high(PS + (p - 6) * 6 + c)
            w[p * 12 + c] = f
            w[p * 12 + 6 + c] = adjoint(p, as_, c, 3 + c)
    for p in range(1, 9):
        for c in range(3):
            if p < 2:
                f = low(PV + 2 * 3 + c)
            elif p < 6:
                f = fv[c, p - 2]
            else:
                f = high(PV + (p - 6) * 3 + c)
            w[VB + (p - 1) * 6 + c] = f
            w[VB + (p - 1) * 6 + 3 + c] = adjoint(p, av, c, c)
        if p < 2:
            r = low(PR + 2)
        elif p < 6:
            r = rho[p - 2]
        else:
            r = high(PR + p - 6)
        live = r > 0.0
        w[CB + p - 1] = jnp.where(live, (0.5 * H) / jnp.where(live, r, 1.0), 0.0)
    for p in range(2, 8):
        for c, base in ((0, LB), (1, MB)):
            m = lam[c, p - 2] if p < 6 else high(PL + (p - 6) * 2 + c)
            w[base + p - 2] = (0.5 * H) * m
    for n in range(188, N):
        w[n] = jnp.zeros((8, 128), jnp.float32)


def lanes():
    return lax.broadcasted_iota(jnp.int32, (8, 128), 1)


def edge_kernel(sc, w, ga, gb, out_a, out_b):
    gy_odd, gz_odd = sc[3], sc[4]
    lane = lanes()

    def group(g, carry):
        for out, up in ((out_a, 1 - gz_odd), (out_b, gz_odd)):
            for t in range(3):
                acc = jnp.zeros((8, 128), jnp.float32)
                for k in range(16):
                    n = g * 16 + k
                    if t == 1:
                        x = w[n]
                    else:
                        x = jnp.where((gy_odd == 1) == (t == 0), ga[n], gb[n])
                    x = pltpu.roll(x, lax.rem(8 * k + 8 * up, 128), 1)
                    acc = jnp.where((lane >= 8 * k) & (lane < 8 * k + 8), x, acc)
                out[t * 12 + g] = acc
        return carry

    lax.fori_loop(0, 12, group, 0)


def rows_diff(x):
    return pltpu.roll(x, 23, 0) - pltpu.roll(x, 1, 0)


def lanes_diff(x):
    return pltpu.roll(x, 255, 1) - pltpu.roll(x, 1, 1)


def one_step(st, kern):
    def velocity(p, carry):
        coef = st[CB + p - 1]
        for q in range(2):
            base = p * 12 + q * 6
            for i in range(3):
                x, y, z = PAIRS[i]
                force = st[base + 12 + x] - st[base - 12 + x]
                force = force + rows_diff(st[base + y]) + lanes_diff(st[base + z])
                n = VB + (p - 1) * 6 + q * 3 + i
                if q == 0:
                    st[n] = st[n] - coef * force
                else:
                    st[n] = st[n] + coef * force
        return carry

    lax.fori_loop(1, 9, velocity, 0)

    def stress(p, carry):
        lam, mu = st[LB + p - 2], st[MB + p - 2]
        traces, diags, shears, vels = [], [], [], []
        for q in range(2):
            v = VB + (p - 1) * 6 + q * 3
            own = [st[v + i] for i in range(3)]
            dx = [st[v + 6 + i] - st[v - 6 + i] for i in range(3)]
            dy = [rows_diff(f) for f in own]
            dz = [lanes_diff(f) for f in own]
            diag = [dx[0], dy[1], dz[2]]
            shear = [dy[2] + dz[1], dx[2] + dz[0], dx[1] + dy[0]]
            trace = diag[0] + diag[1] + diag[2]
            iso = lam * trace
            s = p * 12 + q * 6
            for c in range(3):
                a = iso + (2.0 * mu) * diag[c]
                b = mu * shear[c]
                if q == 0:
                    st[s + c] = st[s + c] - a
                    st[s + 3 + c] = st[s + 3 + c] - b
                else:
                    st[s + c] = st[s + c] + a
                    st[s + 3 + c] = st[s + 3 + c] + b
            cut = lambda f: f[8:16, 0:128]
            traces.append(cut(trace))
            diags.append([cut(f) for f in diag])
            shears.append([cut(f) for f in shear])
            vels.append([cut(f) for f in own])
        dot = lambda pair: (
            pair[0][0] * pair[1][0] + pair[0][1] * pair[1][1] + pair[0][2] * pair[1][2]
        )
        kern[p - 2] += H * dot(vels)
        kern[6 + p - 2] += (0.25 * H) * (traces[0] * traces[1])
        kern[12 + p - 2] += (0.5 * H) * dot(diags) + (0.25 * H) * dot(shears)
        return carry

    lax.fori_loop(2, 8, stress, 0)


def write_faces(st, face):
    lane = lanes()
    for t in range(3):
        for g in range(3):
            acc = jnp.zeros((8, 128), jnp.float32)
            for k in range(8):
                n = g * 8 + k
                face[t * 24 + n] = st[48 + n, 8 * t : 8 * t + 8, 0:128]
                x = st[48 + n, 8 * t : 8 * t + 8, 128:256]
                x = pltpu.roll(x, (8 + 16 * k) % 128, 1)
                acc = jnp.where((lane >= 16 * k) & (lane < 16 * k + 16), x, acc)
            face[72 + t * 3 + g] = acc


def read_faces(sc, ra, rb, st):
    lane = lanes()
    halo = (lane < 8) | (lane >= 120)
    low_is_a = sc[0] == 1
    for low in (True, False):
        first = 0 if low else 96
        pick = low_is_a if low else jnp.logical_not(low_is_a)
        get = lambda n: jnp.where(pick, ra[n], rb[n])
        for t in range(3):
            for g in range(3):
                packed = get(72 + t * 3 + g)
                for k in range(8):
                    n = g * 8 + k
                    st[first + n, 8 * t : 8 * t + 8, 0:128] = get(t * 24 + n)
                    x = pltpu.roll(packed, (120 - 16 * k) % 128, 1)
                    st[first + n, 8 * t : 8 * t + 8, 128:256] = jnp.where(halo, x, 0.0)


def first_kernel(sc, w, ga, gb, za, zb, st, kern, face):
    gy_odd, gz_odd = sc[3], sc[4]
    lane = lanes()

    def group(g, carry):
        for t in range(3):
            a, b = za[t * 12 + g], zb[t * 12 + g]
            low = jnp.where(gz_odd == 1, a, b)
            high = jnp.where(gz_odd == 1, b, a)
            for k in range(16):
                n = g * 16 + k
                if t == 1:
                    x = w[n]
                else:
                    x = jnp.where((gy_odd == 1) == (t == 0), ga[n], gb[n])
                st[n, 8 * t : 8 * t + 8, 0:128] = x
                h = pltpu.roll(high, (128 - 8 * k) % 128, 1)
                l = pltpu.roll(low, (120 - 8 * k) % 128, 1)
                st[n, 8 * t : 8 * t + 8, 128:256] = jnp.where(
                    lane < 8, h, jnp.where(lane >= 120, l, 0.0)
                )
        return carry

    lax.fori_loop(0, 12, group, 0)
    for n in range(18):
        kern[n] = jnp.zeros((8, 128), jnp.float32)
    one_step(st, kern)
    write_faces(st, face)


def carry_over(st_in, kern_in, st, kern):
    def move(n, carry):
        st[n] = st_in[n]
        return carry

    lax.fori_loop(24, 96, move, 0, unroll=4)
    lax.fori_loop(VB, 188, move, 0, unroll=4)
    for n in range(18):
        kern[n] = kern_in[n]


def step_kernel(sc, st_in, kern_in, ra, rb, st, kern, face):
    carry_over(st_in, kern_in, st, kern)
    read_faces(sc, ra, rb, st)
    one_step(st, kern)
    write_faces(st, face)


def last_kernel(sc, st_in, kern_in, ra, rb, dens, modu, st, kern):
    carry_over(st_in, kern_in, st, kern)
    read_faces(sc, ra, rb, st)
    one_step(st, kern)
    off, noff = sc[1], sc[2]
    extent = 4 + noff - off
    for r in range(6):
        row = jnp.minimum(off + r, 5)
        live = r < extent
        dens[r] = jnp.where(live, kern[row], 0.0)
        modu[0, r] = jnp.where(live, kern[6 + row], 0.0)
        modu[1, r] = jnp.where(live, kern[12 + row], 0.0)


def call(kernel, outs, args, scratch=()):
    vmem = pl.BlockSpec(memory_space=pltpu.VMEM)
    return pl.pallas_call(
        kernel,
        out_shape=[jax.ShapeDtypeStruct(s, jnp.float32) for s in outs],
        in_specs=[pl.BlockSpec(memory_space=pltpu.SMEM)] + [vmem] * (len(args) - 1),
        out_specs=[vmem] * len(outs),
        scratch_shapes=[pltpu.VMEM(s, jnp.float32) for s in scratch],
        name=kernel.__name__,
    )(*args)


def shards(fwd_velocity, fwd_stress, density, lame, adj_velocity, adj_stress, offsets):
    blocks = lax.axis_size("grp")
    place = lax.axis_index("grp")
    padded = jnp.concatenate([offsets.astype(jnp.int32), jnp.zeros((1,), jnp.int32)])
    pair = lax.dynamic_slice_in_dim(padded, place, 2, 0)
    spot = jnp.arange(8, dtype=jnp.int32)
    sc = jnp.where(
        spot == 0,
        place % 2,
        jnp.where(spot == 3, lax.axis_index("gy") % 2, lax.axis_index("gz") % 2),
    ).astype(jnp.int32)
    sc = jnp.where(spot == 1, pair[0], jnp.where(spot == 2, pair[1], sc))

    raw = (fwd_velocity, fwd_stress, density, lame, adj_velocity, adj_stress)
    send_a, send_b = call(pack_kernel, [(NP1, 8, 128)] * 2, (sc, *raw))
    recv = both_swaps(send_a, send_b, "grp")
    (win,) = call(window_kernel, [(N, 8, 128)], (sc, *raw, *recv))
    ga, gb = both_swaps(win, win, "gy")
    edges = call(edge_kernel, [(36, 8, 128)] * 2, (sc, win, ga, gb))
    za, zb = both_swaps(*edges, "gz")
    state, kern, face = call(
        first_kernel,
        [(N, 24, 256), (18, 8, 128), (NF, 8, 128)],
        (sc, win, ga, gb, za, zb),
    )
    for _ in range(STEPS - 2):
        recv = both_swaps(face, face, "grp")
        state, kern, face = call(
            step_kernel,
            [(N, 24, 256), (18, 8, 128), (NF, 8, 128)],
            (sc, state, kern, *recv),
        )
    recv = both_swaps(face, face, "grp")
    dens, modu = call(
        last_kernel,
        [(6, 8, 128), (2, 6, 8, 128)],
        (sc, state, kern, *recv),
        [(N, 24, 256), (18, 8, 128)],
    )
    return dens, modu


def solution(mesh):
    return jax.shard_map(
        shards,
        mesh=mesh,
        in_specs=(
            P(None, "grp", "gy", "gz"),
            P(None, "grp", "gy", "gz"),
            P("grp", "gy", "gz"),
            P(None, "grp", "gy", "gz"),
            P(None, "grp", "gy", "gz"),
            P(None, "grp", "gy", "gz"),
            P(),
        ),
        out_specs=(P("grp", "gy", "gz"), P(None, "grp", "gy", "gz")),
        check_vma=False,
    )
```

```python
import functools

import jax
import jax.numpy as jnp
from jax import lax
from jax.experimental import pallas as pl
from jax.experimental.pallas import tpu as pltpu
from jax.sharding import PartitionSpec as P

STEPS = 4
H = 0.15
PAIRS = ((0, 5, 4), (5, 1, 3), (4, 3, 2))

VB, CB, LB, MB = 120, 168, 176, 182
N = 192
PA, PV, PS, PR, PL, NP1 = 0, 36, 45, 69, 72, 76
NF = 81
VMEM_LIMIT = 16 << 20


def swaps(count, first):
    out = []
    for i in range(first, count - 1, 2):
        out += [(i, i + 1), (i + 1, i)]
    return out


def both_swaps(value_a, value_b, axis):
    count = lax.axis_size(axis)
    second = lax.ppermute(value_b, axis, swaps(count, 1))
    first = lax.ppermute(value_a, axis, swaps(count, 0))
    return first, second


def pack_kernel(sc, fv, fs, rho, lam, av, as_, out_a, out_b):
    odd, off = sc[0], sc[1]
    for out, up in ((out_a, 1 - odd), (out_b, odd)):
        for i in range(4):
            row = jnp.maximum(2 * up + i - off, 0)
            for c in range(3):
                out[PA + i * 9 + c] = av[c, row]
            for c in range(6):
                out[PA + i * 9 + 3 + c] = as_[c, row]
                out[PS + i * 6 + c] = fs[c, i]
        for i in range(3):
            for c in range(3):
                out[PV + i * 3 + c] = fv[c, i + up]
            out[PR + i] = rho[i + up]
        for i in range(2):
            for c in range(2):
                out[PL + i * 2 + c] = lam[c, i]


def window_kernel(sc, fv, fs, rho, lam, av, as_, ra, rb, w):
    odd, off, noff = sc[0], sc[1], sc[2]
    low_is_a = odd == 1

    def low(n):
        return jnp.where(low_is_a, ra[n], rb[n])

    def high(n):
        return jnp.where(low_is_a, rb[n], ra[n])

    def adjoint(p, ref, c, slot):
        if p < 2:
            return low(PA + p * 9 + slot)
        if p > 7:
            return high(PA + (p - 6) * 9 + slot)
        j = p - 2
        own = ref[c, jnp.clip(j - off, 0, 5)]
        if j < 2:
            return jnp.where(j < off, low(PA + p * 9 + slot), own)
        if j > 3:
            return jnp.where(j - 4 < noff, own, high(PA + (p - 6) * 9 + slot))
        return own

    for p in range(10):
        for c in range(6):
            if p < 2:
                f = low(PS + (p + 2) * 6 + c)
            elif p < 6:
                f = fs[c, p - 2]
            else:
                f = high(PS + (p - 6) * 6 + c)
            w[p * 12 + c] = f
            w[p * 12 + 6 + c] = adjoint(p, as_, c, 3 + c)
    for p in range(1, 9):
        for c in range(3):
            if p < 2:
                f = low(PV + 2 * 3 + c)
            elif p < 6:
                f = fv[c, p - 2]
            else:
                f = high(PV + (p - 6) * 3 + c)
            w[VB + (p - 1) * 6 + c] = f
            w[VB + (p - 1) * 6 + 3 + c] = adjoint(p, av, c, c)
        if p < 2:
            r = low(PR + 2)
        elif p < 6:
            r = rho[p - 2]
        else:
            r = high(PR + p - 6)
        live = r > 0.0
        w[CB + p - 1] = jnp.where(live, (0.5 * H) / jnp.where(live, r, 1.0), 0.0)
    for p in range(2, 8):
        for c, base in ((0, LB), (1, MB)):
            m = lam[c, p - 2] if p < 6 else high(PL + (p - 6) * 2 + c)
            w[base + p - 2] = (0.5 * H) * m
    for n in range(188, N):
        w[n] = jnp.zeros((8, 128), jnp.float32)


def lanes():
    return lax.broadcasted_iota(jnp.int32, (8, 128), 1)


def edge_kernel(sc, w, ga, gb, out_a, out_b):
    gy_odd, gz_odd = sc[3], sc[4]
    lane = lanes()

    def group(g, carry):
        for out, up in ((out_a, 1 - gz_odd), (out_b, gz_odd)):
            for t in range(3):
                acc = jnp.zeros((8, 128), jnp.float32)
                for k in range(16):
                    n = g * 16 + k
                    if t == 1:
                        x = w[n]
                    else:
                        x = jnp.where((gy_odd == 1) == (t == 0), ga[n], gb[n])
                    x = pltpu.roll(x, lax.rem(8 * k + 8 * up, 128), 1)
                    acc = jnp.where((lane >= 8 * k) & (lane < 8 * k + 8), x, acc)
                out[t * 12 + g] = acc
        return carry

    lax.fori_loop(0, 12, group, 0)


def rows_diff(x):
    return pltpu.roll(x, 23, 0) - pltpu.roll(x, 1, 0)


def lanes_diff(x):
    return pltpu.roll(x, 255, 1) - pltpu.roll(x, 1, 1)


def cut(f):
    return f[8:16, 0:128]


def one_step(coefs, stress_at, v_old, kern_old, v_new, kern, s_new=None):
    for p in range(1, 9):
        coef = coefs[CB + p - 1]
        for q in range(2):
            for i in range(3):
                x, y, z = PAIRS[i]
                force = stress_at(p + 1, q * 6 + x) - stress_at(p - 1, q * 6 + x)
                force = force + rows_diff(stress_at(p, q * 6 + y))
                force = force + lanes_diff(stress_at(p, q * 6 + z))
                n = (p - 1) * 6 + q * 3 + i
                v_new[n] = v_old(n) - coef * force if q == 0 else v_old(n) + coef * force
    last = s_new is None
    keep = cut if last else (lambda f: f)
    own_cut = (lambda f: f) if last else cut
    for p in range(2, 8):
        if not last:
            lam, mu = coefs[LB + p - 2], coefs[MB + p - 2]
        traces, diags, shears, vels = [], [], [], []
        for q in range(2):
            v = (p - 1) * 6 + q * 3
            own = [v_new[v + i] for i in range(3)]
            dx = [keep(v_new[v + 6 + i]) - keep(v_new[v - 6 + i]) for i in range(3)]
            dy = [keep(rows_diff(f)) for f in own]
            dz = [keep(lanes_diff(f)) for f in own]
            diag = [dx[0], dy[1], dz[2]]
            shear = [dy[2] + dz[1], dx[2] + dz[0], dx[1] + dy[0]]
            trace = diag[0] + diag[1] + diag[2]
            if not last:
                iso = lam * trace
                for c in range(3):
                    a = iso + (2.0 * mu) * diag[c]
                    b = mu * shear[c]
                    e = q * 6 + c
                    n = (p - 2) * 12 + e
                    if q == 0:
                        s_new[n] = stress_at(p, e) - a
                        s_new[n + 3] = stress_at(p, e + 3) - b
                    else:
                        s_new[n] = stress_at(p, e) + a
                        s_new[n + 3] = stress_at(p, e + 3) + b
            traces.append(own_cut(trace))
            diags.append([own_cut(f) for f in diag])
            shears.append([own_cut(f) for f in shear])
            vels.append([cut(f) for f in own])
        dot = lambda pair: (
            pair[0][0] * pair[1][0] + pair[0][1] * pair[1][1] + pair[0][2] * pair[1][2]
        )
        new = (
            H * dot(vels),
            (0.25 * H) * (traces[0] * traces[1]),
            (0.5 * H) * dot(diags) + (0.25 * H) * dot(shears),
        )
        for k in range(3):
            n = 6 * k + p - 2
            kern[n] = new[k] if kern_old is None else kern_old[n] + new[k]


def write_faces(s_new, face):
    lane = lanes()
    for t in range(3):
        for g in range(3):
            acc = jnp.zeros((8, 128), jnp.float32)
            for k in range(8):
                n = g * 8 + k
                face[t * 24 + n] = s_new[24 + n, 8 * t : 8 * t + 8, 0:128]
                x = s_new[24 + n, 8 * t : 8 * t + 8, 128:256]
                x = pltpu.roll(x, (8 + 16 * k) % 128, 1)
                acc = jnp.where((lane >= 16 * k) & (lane < 16 * k + 16), x, acc)
            face[72 + t * 3 + g] = acc


def read_faces(sc, ra, rb, halo):
    lane = lanes()
    edge = (lane < 8) | (lane >= 120)
    low_is_a = sc[0] == 1
    for low in (True, False):
        first = 0 if low else 24
        pick = low_is_a if low else jnp.logical_not(low_is_a)
        get = lambda n: jnp.where(pick, ra[n], rb[n])
        for t in range(3):
            for g in range(3):
                packed = get(72 + t * 3 + g)
                for k in range(8):
                    n = g * 8 + k
                    halo[first + n, 8 * t : 8 * t + 8, 0:128] = get(t * 24 + n)
                    x = pltpu.roll(packed, (120 - 16 * k) % 128, 1)
                    halo[first + n, 8 * t : 8 * t + 8, 128:256] = jnp.where(edge, x, 0.0)


def first_kernel(sc, w, ga, gb, za, zb, st, s_new, v_new, kern, face):
    gy_odd, gz_odd = sc[3], sc[4]
    lane = lanes()

    def group(g, carry):
        for t in range(3):
            a, b = za[t * 12 + g], zb[t * 12 + g]
            low = jnp.where(gz_odd == 1, a, b)
            high = jnp.where(gz_odd == 1, b, a)
            for k in range(16):
                n = g * 16 + k
                if t == 1:
                    x = w[n]
                else:
                    x = jnp.where((gy_odd == 1) == (t == 0), ga[n], gb[n])
                st[n, 8 * t : 8 * t + 8, 0:128] = x
                h = pltpu.roll(high, (128 - 8 * k) % 128, 1)
                l = pltpu.roll(low, (120 - 8 * k) % 128, 1)
                st[n, 8 * t : 8 * t + 8, 128:256] = jnp.where(
                    lane < 8, h, jnp.where(lane >= 120, l, 0.0)
                )
        return carry

    lax.fori_loop(0, 12, group, 0)
    one_step(st, lambda p, e: st[p * 12 + e], lambda n: st[VB + n], None, v_new, kern, s_new)
    write_faces(s_new, face)


def with_halo(s_old, halo):
    def stress_at(p, e):
        if p < 2:
            return halo[p * 12 + e]
        if p > 7:
            return halo[24 + (p - 8) * 12 + e]
        return s_old[(p - 2) * 12 + e]

    return stress_at


def step_kernel(sc, st, s_old, v_old, kern_old, ra, rb, s_new, v_new, kern, face, halo):
    read_faces(sc, ra, rb, halo)
    one_step(st, with_halo(s_old, halo), lambda n: v_old[n], kern_old, v_new, kern, s_new)
    write_faces(s_new, face)


def last_kernel(sc, st, s_old, v_old, kern_old, ra, rb, dens, modu, halo, v_new, kern):
    read_faces(sc, ra, rb, halo)
    one_step(st, with_halo(s_old, halo), lambda n: v_old[n], kern_old, v_new, kern)
    off, noff = sc[1], sc[2]
    extent = 4 + noff - off
    for r in range(6):
        row = jnp.minimum(off + r, 5)
        live = r < extent
        dens[r] = jnp.where(live, kern[row], 0.0)
        modu[0, r] = jnp.where(live, kern[6 + row], 0.0)
        modu[1, r] = jnp.where(live, kern[12 + row], 0.0)


def call(kernel, outs, args, scratch=()):
    vmem = pl.BlockSpec(memory_space=pltpu.VMEM)
    return pl.pallas_call(
        kernel,
        out_shape=[jax.ShapeDtypeStruct(s, jnp.float32) for s in outs],
        in_specs=[pl.BlockSpec(memory_space=pltpu.SMEM)] + [vmem] * (len(args) - 1),
        out_specs=[vmem] * len(outs),
        scratch_shapes=[pltpu.VMEM(s, jnp.float32) for s in scratch],
        compiler_params=pltpu.CompilerParams(vmem_limit_bytes=VMEM_LIMIT),
        name=kernel.__name__,
    )(*args)


def shards(fwd_velocity, fwd_stress, density, lame, adj_velocity, adj_stress, offsets):
    blocks = lax.axis_size("grp")
    place = lax.axis_index("grp")
    padded = jnp.concatenate([offsets.astype(jnp.int32), jnp.zeros((1,), jnp.int32)])
    pair = lax.dynamic_slice_in_dim(padded, place, 2, 0)
    spot = jnp.arange(8, dtype=jnp.int32)
    sc = jnp.where(
        spot == 0,
        place % 2,
        jnp.where(spot == 3, lax.axis_index("gy") % 2, lax.axis_index("gz") % 2),
    ).astype(jnp.int32)
    sc = jnp.where(spot == 1, pair[0], jnp.where(spot == 2, pair[1], sc))

    raw = (fwd_velocity, fwd_stress, density, lame, adj_velocity, adj_stress)
    send_a, send_b = call(pack_kernel, [(NP1, 8, 128)] * 2, (sc, *raw))
    recv = both_swaps(send_a, send_b, "grp")
    (win,) = call(window_kernel, [(N, 8, 128)], (sc, *raw, *recv))
    ga, gb = both_swaps(win, win, "gy")
    edges = call(edge_kernel, [(36, 8, 128)] * 2, (sc, win, ga, gb))
    za, zb = both_swaps(*edges, "gz")
    carried = [(72, 24, 256), (48, 24, 256), (18, 8, 128), (NF, 8, 128)]
    state, *moving, face = call(
        first_kernel, [(N, 24, 256)] + carried, (sc, win, ga, gb, za, zb)
    )
    for _ in range(STEPS - 2):
        recv = both_swaps(face, face, "grp")
        *moving, face = call(
            step_kernel, carried, (sc, state, *moving, *recv), [(48, 24, 256)]
        )
    recv = both_swaps(face, face, "grp")
    dens, modu = call(
        last_kernel,
        [(6, 8, 128), (2, 6, 8, 128)],
        (sc, state, *moving, *recv),
        [(48, 24, 256), (48, 24, 256), (18, 8, 128)],
    )
    return dens, modu


def solution(mesh):
    return jax.shard_map(
        shards,
        mesh=mesh,
        in_specs=(
            P(None, "grp", "gy", "gz"),
            P(None, "grp", "gy", "gz"),
            P("grp", "gy", "gz"),
            P(None, "grp", "gy", "gz"),
            P(None, "grp", "gy", "gz"),
            P(None, "grp", "gy", "gz"),
            P(),
        ),
        out_specs=(P("grp", "gy", "gz"), P(None, "grp", "gy", "gz")),
        check_vma=False,
    )
```

```python
import functools

import jax
import jax.numpy as jnp
from jax import lax
from jax.experimental import pallas as pl
from jax.experimental.pallas import tpu as pltpu
from jax.sharding import PartitionSpec as P

STEPS = 4
H = 0.15
PAIRS = ((0, 5, 4), (5, 1, 3), (4, 3, 2))

VB, CB, LB, MB = 120, 168, 176, 182
N = 192
PA, PV, PS, PR, PL, NP1 = 0, 36, 45, 69, 72, 76
ALL12 = list(range(12))
X6 = [0, 5, 4, 6, 11, 10]
DEPTHS = ((8, 4), (4, 2), (1, 0))
VMEM_LIMIT = 16 << 20


def swaps(count, first):
    out = []
    for i in range(first, count - 1, 2):
        out += [(i, i + 1), (i + 1, i)]
    return out


def both_swaps(value_a, value_b, axis):
    count = lax.axis_size(axis)
    second = lax.ppermute(value_b, axis, swaps(count, 1))
    first = lax.ppermute(value_a, axis, swaps(count, 0))
    return first, second


def where_am_i(offsets):
    place = lax.axis_index("grp")
    last = lax.axis_size("grp") - 1
    off = offsets[place]
    noff = jnp.where(place < last, offsets[jnp.minimum(place + 1, last)], 0)
    return (
        lax.rem(place, 2),
        off,
        noff,
        lax.rem(lax.axis_index("gy"), 2),
        lax.rem(lax.axis_index("gz"), 2),
    )


def pack_kernel(offsets, *refs):
    raw, (out_a, out_b), held, sems = refs[:6], refs[6:8], refs[8:14], refs[14]
    copies = [pltpu.make_async_copy(raw[k], held[k], sems.at[k]) for k in range(6)]
    for copy in copies:
        copy.start()
    for copy in copies:
        copy.wait()
    fv, fs, rho, lam, av, as_ = held
    odd, off, _, _, _ = where_am_i(offsets)
    for out, up in ((out_a, 1 - odd), (out_b, odd)):
        for i in range(4):
            row = jnp.maximum(2 * up + i - off, 0)
            for c in range(3):
                out[PA + i * 9 + c] = av[c, row]
            for c in range(6):
                out[PA + i * 9 + 3 + c] = as_[c, row]
                out[PS + i * 6 + c] = fs[c, i]
        for i in range(3):
            for c in range(3):
                out[PV + i * 3 + c] = fv[c, i + up]
            out[PR + i] = rho[i + up]
        for i in range(2):
            for c in range(2):
                out[PL + i * 2 + c] = lam[c, i]


def window_kernel(offsets, fv, fs, rho, lam, av, as_, ra, rb, w):
    odd, off, noff, _, _ = where_am_i(offsets)
    low_is_a = odd == 1

    def low(n):
        return jnp.where(low_is_a, ra[n], rb[n])

    def high(n):
        return jnp.where(low_is_a, rb[n], ra[n])

    def adjoint(p, ref, c, slot):
        if p < 2:
            return low(PA + p * 9 + slot)
        if p > 7:
            return high(PA + (p - 6) * 9 + slot)
        j = p - 2
        own = ref[c, jnp.clip(j - off, 0, 5)]
        if j < 2:
            return jnp.where(j < off, low(PA + p * 9 + slot), own)
        if j > 3:
            return jnp.where(j - 4 < noff, own, high(PA + (p - 6) * 9 + slot))
        return own

    for p in range(10):
        for c in range(6):
            if p < 2:
                f = low(PS + (p + 2) * 6 + c)
            elif p < 6:
                f = fs[c, p - 2]
            else:
                f = high(PS + (p - 6) * 6 + c)
            w[p * 12 + c] = f
            w[p * 12 + 6 + c] = adjoint(p, as_, c, 3 + c)
    for p in range(1, 9):
        for c in range(3):
            if p < 2:
                f = low(PV + 2 * 3 + c)
            elif p < 6:
                f = fv[c, p - 2]
            else:
                f = high(PV + (p - 6) * 3 + c)
            w[VB + (p - 1) * 6 + c] = f
            w[VB + (p - 1) * 6 + 3 + c] = adjoint(p, av, c, c)
        if p < 2:
            r = low(PR + 2)
        elif p < 6:
            r = rho[p - 2]
        else:
            r = high(PR + p - 6)
        live = r > 0.0
        w[CB + p - 1] = jnp.where(live, (0.5 * H) / jnp.where(live, r, 1.0), 0.0)
    for p in range(2, 8):
        for c, base in ((0, LB), (1, MB)):
            m = lam[c, p - 2] if p < 6 else high(PL + (p - 6) * 2 + c)
            w[base + p - 2] = (0.5 * H) * m
    for n in range(188, N):
        w[n] = jnp.zeros((8, 128), jnp.float32)


def lanes():
    return lax.broadcasted_iota(jnp.int32, (8, 128), 1)


def edge_kernel(offsets, w, ga, gb, out_a, out_b):
    _, _, _, gy_odd, gz_odd = where_am_i(offsets)
    lane = lanes()

    def group(g, carry):
        for out, up in ((out_a, 1 - gz_odd), (out_b, gz_odd)):
            for t in range(3):
                acc = jnp.zeros((8, 128), jnp.float32)
                for k in range(16):
                    n = g * 16 + k
                    if t == 1:
                        x = w[n]
                    else:
                        x = jnp.where((gy_odd == 1) == (t == 0), ga[n], gb[n])
                    x = pltpu.roll(x, lax.rem(8 * k + 8 * up, 128), 1)
                    acc = jnp.where((lane >= 8 * k) & (lane < 8 * k + 8), x, acc)
                out[t * 12 + g] = acc
        return carry

    lax.fori_loop(0, 12, group, 0)


def rows_diff(x):
    return pltpu.roll(x, 23, 0) - pltpu.roll(x, 1, 0)


def lanes_diff(x):
    return pltpu.roll(x, 255, 1) - pltpu.roll(x, 1, 1)


def cut(f):
    return f[8:16, 0:128]


def one_step(coefs, stress_at, v_old, kern_old, v_new, kern, s_new=None):
    for p in range(1, 9):
        coef = coefs[CB + p - 1]
        for q in range(2):
            for i in range(3):
                x, y, z = PAIRS[i]
                force = stress_at(p + 1, q * 6 + x) - stress_at(p - 1, q * 6 + x)
                force = force + rows_diff(stress_at(p, q * 6 + y))
                force = force + lanes_diff(stress_at(p, q * 6 + z))
                n = (p - 1) * 6 + q * 3 + i
                v_new[n] = v_old(n) - coef * force if q == 0 else v_old(n) + coef * force
    last = s_new is None
    keep = cut if last else (lambda f: f)
    own_cut = (lambda f: f) if last else cut
    for p in range(2, 8):
        if not last:
            lam, mu = coefs[LB + p - 2], coefs[MB + p - 2]
        traces, diags, shears, vels = [], [], [], []
        for q in range(2):
            v = (p - 1) * 6 + q * 3
            own = [v_new[v + i] for i in range(3)]
            dx = [keep(v_new[v + 6 + i]) - keep(v_new[v - 6 + i]) for i in range(3)]
            dy = [keep(rows_diff(f)) for f in own]
            dz = [keep(lanes_diff(f)) for f in own]
            diag = [dx[0], dy[1], dz[2]]
            shear = [dy[2] + dz[1], dx[2] + dz[0], dx[1] + dy[0]]
            trace = diag[0] + diag[1] + diag[2]
            if not last:
                iso = lam * trace
                for c in range(3):
                    a = iso + (2.0 * mu) * diag[c]
                    b = mu * shear[c]
                    e = q * 6 + c
                    n = (p - 2) * 12 + e
                    if q == 0:
                        s_new[n] = stress_at(p, e) - a
                        s_new[n + 3] = stress_at(p, e + 3) - b
                    else:
                        s_new[n] = stress_at(p, e) + a
                        s_new[n + 3] = stress_at(p, e + 3) + b
            traces.append(own_cut(trace))
            diags.append([own_cut(f) for f in diag])
            shears.append([own_cut(f) for f in shear])
            vels.append([cut(f) for f in own])
        dot = lambda pair: (
            pair[0][0] * pair[1][0] + pair[0][1] * pair[1][1] + pair[0][2] * pair[1][2]
        )
        new = (
            H * dot(vels),
            (0.25 * H) * (traces[0] * traces[1]),
            (0.5 * H) * dot(diags) + (0.25 * H) * dot(shears),
        )
        for k in range(3):
            n = 6 * k + p - 2
            kern[n] = new[k] if kern_old is None else kern_old[n] + new[k]


def row_groups(entries, m):
    size = 4 // m
    return [entries[k : k + size] for k in range(0, len(entries), size)]


def face_blocks(depths):
    blocks = [(1, "own", [e]) for e in ALL12] + [(2, "own", [e]) for e in X6]
    for dx, entries, m in ((1, ALL12, depths[0]), (2, X6, depths[1])):
        if m == 8:
            blocks += [(dx, side, [e]) for e in entries for side in ("low", "high")]
        elif m:
            blocks += [(dx, m, group) for group in row_groups(entries, m)]
    return blocks


def face_tiles(depths):
    count = len(face_blocks(depths))
    return count + -(-count // 8)


def write_faces(odd, depths, s_new, face_a, face_b):
    lane = lanes()
    row = lax.broadcasted_iota(jnp.int32, (8, 256), 0)
    blocks = face_blocks(depths)
    count = len(blocks)
    for face, up in ((face_a, 1 - odd), (face_b, odd)):
        first = {1: (2 + up) * 12, 2: (3 - up) * 12}
        acc = None
        for j, (dx, halo, entries) in enumerate(blocks):
            at = lambda e: first[dx] + e
            if halo == "own":
                x = s_new[at(entries[0]), 8:16, :]
            elif halo == "low":
                x = s_new[at(entries[0]), 0:8, :]
            elif halo == "high":
                x = s_new[at(entries[0]), 16:24, :]
            else:
                m, x = halo, None
                for k, e in enumerate(entries):
                    c = jnp.where(row < 4, s_new[at(e), 16:24, :], s_new[at(e), 0:8, :])
                    if m < 4:
                        c = pltpu.roll(c, (m + 2 * m * k) % 8, 0)
                    x = c if x is None else jnp.where(row < 2 * m * k, x, c)
            face[j] = x[:, 0:128]
            k = j % 8
            h = pltpu.roll(x[:, 128:256], (8 + 16 * k) % 128, 1)
            acc = h if k == 0 else jnp.where(lane < 16 * k, acc, h)
            if k == 7 or j == count - 1:
                face[count + j // 8] = acc


def read_faces(odd, depths, ra, rb, halo):
    lane = lanes()
    edge = (lane < 8) | (lane >= 120)
    low_is_a = odd == 1
    blocks = face_blocks(depths)
    count = len(blocks)
    for low in (True, False):
        first = {1: 12 if low else 24, 2: 0 if low else 36}
        pick = low_is_a if low else jnp.logical_not(low_is_a)
        get = lambda n: jnp.where(pick, ra[n], rb[n])
        packed = None
        for j, (dx, kind, entries) in enumerate(blocks):
            k = j % 8
            if k == 0:
                packed = get(count + j // 8)
            h = pltpu.roll(packed, (120 - 16 * k) % 128, 1)
            x = jnp.concatenate([get(j), jnp.where(edge, h, 0.0)], axis=1)
            if kind in ("own", "low", "high"):
                r = {"low": 0, "own": 8, "high": 16}[kind]
                halo[first[dx] + entries[0], r : r + 8, :] = x
            else:
                m = kind
                for i, e in enumerate(entries):
                    c = x if m == 4 else pltpu.roll(x, (16 - m - 2 * m * i) % 8, 0)
                    halo[first[dx] + e, 0:8, :] = c
                    halo[first[dx] + e, 16:24, :] = c
        if depths[1] == 0:
            for e in X6:
                halo[first[2] + e, 0:8, :] = jnp.zeros((8, 256), jnp.float32)
                halo[first[2] + e, 16:24, :] = jnp.zeros((8, 256), jnp.float32)


def first_kernel(depths, offsets, w, ga, gb, za, zb, st, s_new, v_new, kern, face_a, face_b):
    odd, _, _, gy_odd, gz_odd = where_am_i(offsets)
    lane = lanes()

    def group(g, carry):
        for t in range(3):
            a, b = za[t * 12 + g], zb[t * 12 + g]
            low = jnp.where(gz_odd == 1, a, b)
            high = jnp.where(gz_odd == 1, b, a)
            for k in range(16):
                n = g * 16 + k
                if t == 1:
                    x = w[n]
                else:
                    x = jnp.where((gy_odd == 1) == (t == 0), ga[n], gb[n])
                st[n, 8 * t : 8 * t + 8, 0:128] = x
                h = pltpu.roll(high, (128 - 8 * k) % 128, 1)
                l = pltpu.roll(low, (120 - 8 * k) % 128, 1)
                st[n, 8 * t : 8 * t + 8, 128:256] = jnp.where(
                    lane < 8, h, jnp.where(lane >= 120, l, 0.0)
                )
        return carry

    lax.fori_loop(0, 12, group, 0)
    one_step(st, lambda p, e: st[p * 12 + e], lambda n: st[VB + n], None, v_new, kern, s_new)
    write_faces(odd, depths, s_new, face_a, face_b)


def with_halo(s_old, halo):
    def stress_at(p, e):
        if p < 2:
            return halo[p * 12 + e]
        if p > 7:
            return halo[24 + (p - 8) * 12 + e]
        return s_old[(p - 2) * 12 + e]

    return stress_at


def step_kernel(
    before, after, offsets, st, s_old, v_old, kern_old, ra, rb, s_new, v_new, kern, face_a, face_b, halo
):
    odd = where_am_i(offsets)[0]
    read_faces(odd, before, ra, rb, halo)
    one_step(st, with_halo(s_old, halo), lambda n: v_old[n], kern_old, v_new, kern, s_new)
    write_faces(odd, after, s_new, face_a, face_b)


def last_kernel(
    before, offsets, st, s_old, v_old, kern_old, ra, rb, dens, modu, halo, v_new, kern
):
    odd, off, noff, _, _ = where_am_i(offsets)
    read_faces(odd, before, ra, rb, halo)
    one_step(st, with_halo(s_old, halo), lambda n: v_old[n], kern_old, v_new, kern)
    extent = 4 + noff - off
    for r in range(6):
        row = jnp.minimum(off + r, 5)
        live = r < extent
        dens[r] = jnp.where(live, kern[row], 0.0)
        modu[0, r] = jnp.where(live, kern[6 + row], 0.0)
        modu[1, r] = jnp.where(live, kern[12 + row], 0.0)


def call(kernel, name, outs, args, scratch=(), space=pltpu.VMEM):
    vmem = pl.BlockSpec(memory_space=pltpu.VMEM)
    return pl.pallas_call(
        kernel,
        out_shape=[jax.ShapeDtypeStruct(s, jnp.float32) for s in outs],
        in_specs=[pl.BlockSpec(memory_space=pltpu.SMEM)]
        + [pl.BlockSpec(memory_space=space)] * (len(args) - 1),
        out_specs=[vmem] * len(outs),
        scratch_shapes=[pltpu.VMEM(s, jnp.float32) if isinstance(s, tuple) else s for s in scratch],
        compiler_params=pltpu.CompilerParams(vmem_limit_bytes=VMEM_LIMIT),
        name=name,
    )(*args)


def shards(fwd_velocity, fwd_stress, density, lame, adj_velocity, adj_stress, offsets):
    raw = (fwd_velocity, fwd_stress, density, lame, adj_velocity, adj_stress)
    raw = [pltpu.with_memory_space_constraint(a, pltpu.HBM) for a in raw]
    send_a, send_b, *held = call(
        pack_kernel,
        "pack",
        [(NP1, 8, 128)] * 2 + [a.shape for a in raw],
        (offsets, *raw),
        [pltpu.SemaphoreType.DMA((6,))],
        pltpu.HBM,
    )
    recv = both_swaps(send_a, send_b, "grp")
    (win,) = call(window_kernel, "window", [(N, 8, 128)], (offsets, *held, *recv))
    ga, gb = both_swaps(win, win, "gy")
    edges = call(edge_kernel, "edge", [(36, 8, 128)] * 2, (offsets, win, ga, gb))
    za, zb = both_swaps(*edges, "gz")
    carried = [(72, 24, 256), (48, 24, 256), (18, 8, 128)]
    faces = lambda k: [(face_tiles(DEPTHS[k]), 8, 128)] * 2
    state, *moving, face_a, face_b = call(
        functools.partial(first_kernel, DEPTHS[0]),
        "first",
        [(N, 24, 256)] + carried + faces(0),
        (offsets, win, ga, gb, za, zb),
    )
    for k in range(STEPS - 2):
        recv = both_swaps(face_a, face_b, "grp")
        *moving, face_a, face_b = call(
            functools.partial(step_kernel, DEPTHS[k], DEPTHS[k + 1]),
            "step",
            carried + faces(k + 1),
            (offsets, state, *moving, *recv),
            [(48, 24, 256)],
        )
    recv = both_swaps(face_a, face_b, "grp")
    dens, modu = call(
        functools.partial(last_kernel, DEPTHS[STEPS - 2]),
        "last",
        [(6, 8, 128), (2, 6, 8, 128)],
        (offsets, state, *moving, *recv),
        [(48, 24, 256), (48, 24, 256), (18, 8, 128)],
    )
    return dens, modu


def solution(mesh):
    return jax.shard_map(
        shards,
        mesh=mesh,
        in_specs=(
            P(None, "grp", "gy", "gz"),
            P(None, "grp", "gy", "gz"),
            P("grp", "gy", "gz"),
            P(None, "grp", "gy", "gz"),
            P(None, "grp", "gy", "gz"),
            P(None, "grp", "gy", "gz"),
            P(),
        ),
        out_specs=(P("grp", "gy", "gz"), P(None, "grp", "gy", "gz")),
        check_vma=False,
    )
```

```python
import jax
import jax.numpy as jnp
from jax import lax
from jax.experimental import pallas as pl
from jax.experimental.pallas import tpu as pltpu
from jax.sharding import PartitionSpec as P

H = 0.15
PAIRS = ((0, 5, 4), (5, 1, 3), (4, 3, 2))

VB, CB, LB, MB = 120, 168, 176, 182
N = 192
PA, PV, PS, PR, PL, NP1 = 0, 36, 45, 69, 72, 76
ALL12 = list(range(12))
X6 = [0, 5, 4, 6, 11, 10]
MID = [
    ([("s", 1, e) for e in ALL12], 5),
    (
        [("s", dx, e) for dx in (2, 3) for e in ALL12]
        + [("v", 2, e) for e in range(6)]
        + [("c", 2, 0), ("l", 1, 0), ("m", 1, 0)],
        4,
    ),
    (
        [("s", 4, e) for e in X6]
        + [("v", 3, e) for e in range(6)]
        + [("c", 3, 0), ("l", 2, 0), ("m", 2, 0)],
        2,
    ),
]
LAST = [([("s", 1, e) for e in ALL12], 1), ([("s", 2, e) for e in X6], 0)]
VMEM_LIMIT = 16 << 20


def swaps(count, first):
    out = []
    for i in range(first, count - 1, 2):
        out += [(i, i + 1), (i + 1, i)]
    return out


def both_swaps(value_a, value_b, axis):
    count = lax.axis_size(axis)
    second = lax.ppermute(value_b, axis, swaps(count, 1))
    first = lax.ppermute(value_a, axis, swaps(count, 0))
    return first, second


def where_am_i(offsets):
    place = lax.axis_index("grp")
    last = lax.axis_size("grp") - 1
    off = offsets[place]
    noff = jnp.where(place < last, offsets[jnp.minimum(place + 1, last)], 0)
    return (
        lax.rem(place, 2),
        off,
        noff,
        lax.rem(lax.axis_index("gy"), 2),
        lax.rem(lax.axis_index("gz"), 2),
    )


def pack_kernel(offsets, *refs):
    raw, (out_a, out_b), held, sems = refs[:6], refs[6:8], refs[8:14], refs[14]
    copies = [pltpu.make_async_copy(raw[k], held[k], sems.at[k]) for k in range(6)]
    for copy in copies:
        copy.start()
    for copy in copies:
        copy.wait()
    fv, fs, rho, lam, av, as_ = held
    odd, off, _, _, _ = where_am_i(offsets)
    for out, up in ((out_a, 1 - odd), (out_b, odd)):
        for i in range(4):
            row = jnp.maximum(2 * up + i - off, 0)
            for c in range(3):
                out[PA + i * 9 + c] = av[c, row]
            for c in range(6):
                out[PA + i * 9 + 3 + c] = as_[c, row]
                out[PS + i * 6 + c] = fs[c, i]
        for i in range(3):
            for c in range(3):
                out[PV + i * 3 + c] = fv[c, i + up]
            out[PR + i] = rho[i + up]
        for i in range(2):
            for c in range(2):
                out[PL + i * 2 + c] = lam[c, i]


def window_kernel(offsets, fv, fs, rho, lam, av, as_, ra, rb, w):
    odd, off, noff, _, _ = where_am_i(offsets)
    low_is_a = odd == 1

    def low(n):
        return jnp.where(low_is_a, ra[n], rb[n])

    def high(n):
        return jnp.where(low_is_a, rb[n], ra[n])

    def adjoint(p, ref, c, slot):
        if p < 2:
            return low(PA + p * 9 + slot)
        if p > 7:
            return high(PA + (p - 6) * 9 + slot)
        j = p - 2
        own = ref[c, jnp.clip(j - off, 0, 5)]
        if j < 2:
            return jnp.where(j < off, low(PA + p * 9 + slot), own)
        if j > 3:
            return jnp.where(j - 4 < noff, own, high(PA + (p - 6) * 9 + slot))
        return own

    for p in range(10):
        for c in range(6):
            if p < 2:
                f = low(PS + (p + 2) * 6 + c)
            elif p < 6:
                f = fs[c, p - 2]
            else:
                f = high(PS + (p - 6) * 6 + c)
            w[p * 12 + c] = f
            w[p * 12 + 6 + c] = adjoint(p, as_, c, 3 + c)
    for p in range(1, 9):
        for c in range(3):
            if p < 2:
                f = low(PV + 2 * 3 + c)
            elif p < 6:
                f = fv[c, p - 2]
            else:
                f = high(PV + (p - 6) * 3 + c)
            w[VB + (p - 1) * 6 + c] = f
            w[VB + (p - 1) * 6 + 3 + c] = adjoint(p, av, c, c)
        if p < 2:
            r = low(PR + 2)
        elif p < 6:
            r = rho[p - 2]
        else:
            r = high(PR + p - 6)
        live = r > 0.0
        w[CB + p - 1] = jnp.where(live, (0.5 * H) / jnp.where(live, r, 1.0), 0.0)
    for p in range(2, 8):
        for c, base in ((0, LB), (1, MB)):
            m = lam[c, p - 2] if p < 6 else high(PL + (p - 6) * 2 + c)
            w[base + p - 2] = (0.5 * H) * m
    for n in range(188, N):
        w[n] = jnp.zeros((8, 128), jnp.float32)


def lanes():
    return lax.broadcasted_iota(jnp.int32, (8, 128), 1)


def edge_kernel(offsets, w, ga, gb, out_a, out_b):
    _, _, _, gy_odd, gz_odd = where_am_i(offsets)
    lane = lanes()

    def group(g, carry):
        for out, up in ((out_a, 1 - gz_odd), (out_b, gz_odd)):
            for t in range(3):
                acc = jnp.zeros((8, 128), jnp.float32)
                for k in range(16):
                    n = g * 16 + k
                    if t == 1:
                        x = w[n]
                    else:
                        x = jnp.where((gy_odd == 1) == (t == 0), ga[n], gb[n])
                    x = pltpu.roll(x, lax.rem(8 * k + 8 * up, 128), 1)
                    acc = jnp.where((lane >= 8 * k) & (lane < 8 * k + 8), x, acc)
                out[t * 12 + g] = acc
        return carry

    lax.fori_loop(0, 12, group, 0)


def rows_diff(x):
    return pltpu.roll(x, 23, 0) - pltpu.roll(x, 1, 0)


def lanes_diff(x):
    return pltpu.roll(x, 255, 1) - pltpu.roll(x, 1, 1)


def cut(f):
    return f[8:16, 0:128]


def cut(f):
    return f[8:16, 0:128]


def velocity_step(planes, coef_at, stress_at, v_old, v_new, base):
    for p in planes:
        coef = coef_at(p)
        for q in range(2):
            for i in range(3):
                x, y, z = PAIRS[i]
                force = stress_at(p + 1, q * 6 + x) - stress_at(p - 1, q * 6 + x)
                force = force + rows_diff(stress_at(p, q * 6 + y))
                force = force + lanes_diff(stress_at(p, q * 6 + z))
                e = q * 3 + i
                step = coef * force
                old = v_old(p, e)
                v_new[(p - base) * 6 + e] = old - step if q == 0 else old + step


def stress_step(planes, lame_at, stress_at, v, v_base, kern_old, kern, s_new=None, s_base=2):
    last = s_new is None
    keep = cut if last else (lambda f: f)
    own_cut = (lambda f: f) if last else cut
    for p in planes:
        if not last:
            lam, mu = lame_at(p)
        traces, diags, shears, vels = [], [], [], []
        for q in range(2):
            n = (p - v_base) * 6 + q * 3
            own = [v[n + i] for i in range(3)]
            dx = [keep(v[n + 6 + i]) - keep(v[n - 6 + i]) for i in range(3)]
            dy = [keep(rows_diff(f)) for f in own]
            dz = [keep(lanes_diff(f)) for f in own]
            diag = [dx[0], dy[1], dz[2]]
            shear = [dy[2] + dz[1], dx[2] + dz[0], dx[1] + dy[0]]
            trace = diag[0] + diag[1] + diag[2]
            if not last:
                iso = lam * trace
                for c in range(3):
                    a = iso + (2.0 * mu) * diag[c]
                    b = mu * shear[c]
                    e = q * 6 + c
                    n = (p - s_base) * 12 + e
                    if q == 0:
                        s_new[n] = stress_at(p, e) - a
                        s_new[n + 3] = stress_at(p, e + 3) - b
                    else:
                        s_new[n] = stress_at(p, e) + a
                        s_new[n + 3] = stress_at(p, e + 3) + b
            if 2 <= p < 8:
                traces.append(own_cut(trace))
                diags.append([own_cut(f) for f in diag])
                shears.append([own_cut(f) for f in shear])
                vels.append([cut(f) for f in own])
        if not 2 <= p < 8:
            continue
        dot = lambda pair: (
            pair[0][0] * pair[1][0] + pair[0][1] * pair[1][1] + pair[0][2] * pair[1][2]
        )
        new = (
            H * dot(vels),
            (0.25 * H) * (traces[0] * traces[1]),
            (0.5 * H) * dot(diags) + (0.25 * H) * dot(shears),
        )
        for k in range(3):
            n = 6 * k + p - 2
            kern[n] = new[k] if kern_old is None else kern_old[n] + new[k]


def face_blocks(spec):
    blocks = [("own", [item]) for items, _ in spec for item in items]
    for items, m in spec:
        if m == 5:
            blocks += [(4, [item]) for item in items]
            blocks += [(5, items[k : k + 4]) for k in range(0, len(items), 4)]
        elif m:
            size = 4 // m
            blocks += [(m, items[k : k + size]) for k in range(0, len(items), size)]
    return blocks


def face_tiles(spec):
    count = len(face_blocks(spec))
    return count + -(-count // 8)


def face_places(spec):
    items = [item for group, _ in spec for item in group]
    return {item: k for k, item in enumerate(items)}, len(items)


def write_faces(odd, spec, st, s_new, v_new, face_a, face_b):
    lane = lanes()
    row = lax.broadcasted_iota(jnp.int32, (8, 256), 0)
    blocks = face_blocks(spec)
    count = len(blocks)
    for face, up in ((face_a, 1 - odd), (face_b, odd)):

        def source(item):
            kind, dx, e = item
            p = (3 + dx) + up * (3 - 2 * dx)
            if kind == "s":
                return s_new, (p - 2) * 12 + e
            if kind == "v":
                return v_new, (p - 1) * 6 + e
            return st, {"c": CB - 1, "l": LB - 2, "m": MB - 2}[kind] + p

        acc = None
        for j, (kind, items) in enumerate(blocks):
            if kind == "own":
                ref, n = source(items[0])
                x = ref[n, 8:16, :]
            else:
                m, x = kind, None
                for k, item in enumerate(items):
                    ref, n = source(item)
                    low, high = ref[n, 0:8, :], ref[n, 16:24, :]
                    if m == 5:
                        c = pltpu.roll(jnp.where(row == 3, low, high), (2 * k + 5) % 8, 0)
                        x = c if x is None else jnp.where(row < 2 * k, x, c)
                        continue
                    c = jnp.where(row < 4, high, low)
                    if m < 4:
                        c = pltpu.roll(c, (m + 2 * m * k) % 8, 0)
                    x = c if x is None else jnp.where(row < 2 * m * k, x, c)
            face[j] = x[:, 0:128]
            k = j % 8
            h = pltpu.roll(x[:, 128:256], (8 + 16 * k) % 128, 1)
            acc = h if k == 0 else jnp.where(lane < 16 * k, acc, h)
            if k == 7 or j == count - 1:
                face[count + j // 8] = acc


def read_faces(odd, spec, ra, rb, halo):
    lane = lanes()
    edge = (lane < 8) | (lane >= 120)
    low_is_a = odd == 1
    blocks = face_blocks(spec)
    count = len(blocks)
    place, total = face_places(spec)
    for low in (True, False):
        first = 0 if low else total
        pick = low_is_a if low else jnp.logical_not(low_is_a)
        get = lambda n: jnp.where(pick, ra[n], rb[n])
        packed = None
        for j, (kind, items) in enumerate(blocks):
            k = j % 8
            if k == 0:
                packed = get(count + j // 8)
            h = pltpu.roll(packed, (120 - 16 * k) % 128, 1)
            x = jnp.concatenate([get(j), jnp.where(edge, h, 0.0)], axis=1)
            for i, item in enumerate(items):
                n = first + place[item]
                if kind == "own":
                    halo[n, 8:16, :] = x
                elif kind == 5:
                    c = pltpu.roll(x, (11 - 2 * i) % 8, 0)
                    halo[n, 3:4, :] = c[3:4, :]
                    halo[n, 20:21, :] = c[4:5, :]
                else:
                    c = x if kind == 4 else pltpu.roll(x, (16 - kind - 2 * kind * i) % 8, 0)
                    halo[n, 0:8, :] = c
                    halo[n, 16:24, :] = c
        for items, m in spec:
            for item in items if m == 0 else ():
                halo[first + place[item], 0:8, :] = jnp.zeros((8, 256), jnp.float32)
                halo[first + place[item], 16:24, :] = jnp.zeros((8, 256), jnp.float32)


def first_kernel(offsets, w, ga, gb, za, zb, st, s_new, v_new, kern, face_a, face_b):
    odd, _, _, gy_odd, gz_odd = where_am_i(offsets)
    lane = lanes()

    def group(g, carry):
        for t in range(3):
            a, b = za[t * 12 + g], zb[t * 12 + g]
            low = jnp.where(gz_odd == 1, a, b)
            high = jnp.where(gz_odd == 1, b, a)
            for k in range(16):
                n = g * 16 + k
                if t == 1:
                    x = w[n]
                else:
                    x = jnp.where((gy_odd == 1) == (t == 0), ga[n], gb[n])
                st[n, 8 * t : 8 * t + 8, 0:128] = x
                h = pltpu.roll(high, (128 - 8 * k) % 128, 1)
                l = pltpu.roll(low, (120 - 8 * k) % 128, 1)
                st[n, 8 * t : 8 * t + 8, 128:256] = jnp.where(
                    lane < 8, h, jnp.where(lane >= 120, l, 0.0)
                )
        return carry

    lax.fori_loop(0, 12, group, 0)
    stress_at = lambda p, e: st[p * 12 + e]
    velocity_step(
        range(1, 9),
        lambda p: st[CB + p - 1],
        stress_at,
        lambda p, e: st[VB + (p - 1) * 6 + e],
        v_new,
        1,
    )
    lame_at = lambda p: (st[LB + p - 2], st[MB + p - 2])
    stress_step(range(2, 8), lame_at, stress_at, v_new, 1, None, kern, s_new)
    write_faces(odd, MID, st, s_new, v_new, face_a, face_b)


def reader(spec, halo):
    place, total = face_places(spec)

    def at(kind, p, first, e, inside):
        if first <= p <= 9 - first:
            return inside()
        low = p < first
        dx = 2 - p if low else p - 7
        return halo[place[(kind, dx, e)] + (0 if low else total)]

    return at


def middle_kernel(
    offsets, st, s_old, v_old, kern_old, ra, rb, s_new, v_new, kern, face_a, face_b, halo, s_mid, v_mid
):
    odd = where_am_i(offsets)[0]
    read_faces(odd, MID, ra, rb, halo)
    at = reader(MID, halo)
    coef_at = lambda p: at("c", p, 1, 0, lambda: st[CB + p - 1])
    lame_at = lambda p: (
        at("l", p, 2, 0, lambda: st[LB + p - 2]),
        at("m", p, 2, 0, lambda: st[MB + p - 2]),
    )
    stress_at = lambda p, e: at("s", p, 2, e, lambda: s_old[(p - 2) * 12 + e])
    v_at = lambda p, e: at("v", p, 1, e, lambda: v_old[(p - 1) * 6 + e])
    velocity_step(range(-1, 11), coef_at, stress_at, v_at, v_mid, -1)
    stress_step(range(0, 10), lame_at, stress_at, v_mid, -1, kern_old, kern, s_mid, 0)
    stress_mid = lambda p, e: s_mid[p * 12 + e]
    v_at_mid = lambda p, e: v_mid[(p + 1) * 6 + e]
    velocity_step(range(1, 9), coef_at, stress_mid, v_at_mid, v_new, 1)
    stress_step(range(2, 8), lame_at, stress_mid, v_new, 1, kern, kern, s_new)
    write_faces(odd, LAST, st, s_new, v_new, face_a, face_b)


def last_kernel(
    offsets, st, s_old, v_old, kern_old, ra, rb, dens, modu, halo, v_new, kern
):
    odd, off, noff, _, _ = where_am_i(offsets)
    read_faces(odd, LAST, ra, rb, halo)
    at = reader(LAST, halo)
    stress_at = lambda p, e: at("s", p, 2, e, lambda: s_old[(p - 2) * 12 + e])
    velocity_step(
        range(1, 9),
        lambda p: st[CB + p - 1],
        stress_at,
        lambda p, e: v_old[(p - 1) * 6 + e],
        v_new,
        1,
    )
    stress_step(range(2, 8), None, stress_at, v_new, 1, kern_old, kern)
    extent = 4 + noff - off
    for r in range(6):
        row = jnp.minimum(off + r, 5)
        live = r < extent
        dens[r] = jnp.where(live, kern[row], 0.0)
        modu[0, r] = jnp.where(live, kern[6 + row], 0.0)
        modu[1, r] = jnp.where(live, kern[12 + row], 0.0)


def call(kernel, name, outs, args, scratch=(), space=pltpu.VMEM):
    vmem = pl.BlockSpec(memory_space=pltpu.VMEM)
    return pl.pallas_call(
        kernel,
        out_shape=[jax.ShapeDtypeStruct(s, jnp.float32) for s in outs],
        in_specs=[pl.BlockSpec(memory_space=pltpu.SMEM)]
        + [pl.BlockSpec(memory_space=space)] * (len(args) - 1),
        out_specs=[vmem] * len(outs),
        scratch_shapes=[pltpu.VMEM(s, jnp.float32) if isinstance(s, tuple) else s for s in scratch],
        compiler_params=pltpu.CompilerParams(vmem_limit_bytes=VMEM_LIMIT),
        name=name,
    )(*args)


def shards(fwd_velocity, fwd_stress, density, lame, adj_velocity, adj_stress, offsets):
    raw = (fwd_velocity, fwd_stress, density, lame, adj_velocity, adj_stress)
    raw = [pltpu.with_memory_space_constraint(a, pltpu.HBM) for a in raw]
    send_a, send_b, *held = call(
        pack_kernel,
        "pack",
        [(NP1, 8, 128)] * 2 + [a.shape for a in raw],
        (offsets, *raw),
        [pltpu.SemaphoreType.DMA((6,))],
        pltpu.HBM,
    )
    recv = both_swaps(send_a, send_b, "grp")
    (win,) = call(window_kernel, "window", [(N, 8, 128)], (offsets, *held, *recv))
    ga, gb = both_swaps(win, win, "gy")
    edges = call(edge_kernel, "edge", [(36, 8, 128)] * 2, (offsets, win, ga, gb))
    za, zb = both_swaps(*edges, "gz")
    carried = [(72, 24, 256), (48, 24, 256), (18, 8, 128)]
    faces = lambda spec: [(face_tiles(spec), 8, 128)] * 2
    halos = lambda spec: (2 * face_places(spec)[1], 24, 256)
    state, *moving, face_a, face_b = call(
        first_kernel,
        "first",
        [(N, 24, 256)] + carried + faces(MID),
        (offsets, win, ga, gb, za, zb),
    )
    recv = both_swaps(face_a, face_b, "grp")
    *moving, face_a, face_b = call(
        middle_kernel,
        "middle",
        carried + faces(LAST),
        (offsets, state, *moving, *recv),
        [halos(MID), (120, 24, 256), (72, 24, 256)],
    )
    recv = both_swaps(face_a, face_b, "grp")
    dens, modu = call(
        last_kernel,
        "last",
        [(6, 8, 128), (2, 6, 8, 128)],
        (offsets, state, *moving, *recv),
        [halos(LAST), (48, 24, 256), (18, 8, 128)],
    )
    return dens, modu


def solution(mesh):
    return jax.shard_map(
        shards,
        mesh=mesh,
        in_specs=(
            P(None, "grp", "gy", "gz"),
            P(None, "grp", "gy", "gz"),
            P("grp", "gy", "gz"),
            P(None, "grp", "gy", "gz"),
            P(None, "grp", "gy", "gz"),
            P(None, "grp", "gy", "gz"),
            P(),
        ),
        out_specs=(P("grp", "gy", "gz"), P(None, "grp", "gy", "gz")),
        check_vma=False,
    )
```

```python
import jax
import jax.numpy as jnp
from jax import lax
from jax.experimental import pallas as pl
from jax.experimental.pallas import tpu as pltpu
from jax.sharding import PartitionSpec as P

H = 0.15
PAIRS = ((0, 5, 4), (5, 1, 3), (4, 3, 2))

EB, VB, CB, LB, MB, N = 96, 108, 156, 164, 170, 176
PA, PV, PS, PR, PL, NP1 = 0, 30, 39, 60, 63, 67
X3 = [0, 5, 4]
ALL12 = list(range(12))
X6 = [0, 5, 4, 6, 11, 10]


def entry_s(p, e):
    if 1 <= p <= 8:
        return (p - 1) * 12 + e
    return EB + (6 if p == 9 else 0) + X6.index(e)


MID = [
    ([("s", 1, e) for e in ALL12], 5),
    (
        [("s", dx, e) for dx in (2, 3) for e in ALL12]
        + [("v", 2, e) for e in range(6)]
        + [("c", 2, 0), ("l", 1, 0), ("m", 1, 0)],
        4,
    ),
    (
        [("s", 4, e) for e in X6]
        + [("v", 3, e) for e in range(6)]
        + [("c", 3, 0), ("l", 2, 0), ("m", 2, 0)],
        2,
    ),
]
LAST = [([("s", 1, e) for e in ALL12], 1), ([("s", 2, e) for e in X6], 0)]
VMEM_LIMIT = 16 << 20


def swaps(count, first):
    out = []
    for i in range(first, count - 1, 2):
        out += [(i, i + 1), (i + 1, i)]
    return out


def both_swaps(value_a, value_b, axis):
    count = lax.axis_size(axis)
    second = lax.ppermute(value_b, axis, swaps(count, 1))
    first = lax.ppermute(value_a, axis, swaps(count, 0))
    return first, second


def where_am_i(offsets):
    place = lax.axis_index("grp")
    last = lax.axis_size("grp") - 1
    off = offsets[place]
    noff = jnp.where(place < last, offsets[jnp.minimum(place + 1, last)], 0)
    return (
        lax.rem(place, 2),
        off,
        noff,
        lax.rem(lax.axis_index("gy"), 2),
        lax.rem(lax.axis_index("gz"), 2),
    )


def pack_kernel(offsets, *refs):
    raw, (out_a, out_b), held, sems = refs[:6], refs[6:8], refs[8:14], refs[14]
    copies = [pltpu.make_async_copy(raw[k], held[k], sems.at[k]) for k in range(6)]
    for copy in copies:
        copy.start()
    for copy in copies:
        copy.wait()
    fv, fs, rho, lam, av, as_ = held
    odd, off, _, _, _ = where_am_i(offsets)
    for out, up in ((out_a, 1 - odd), (out_b, odd)):
        for k in range(4):
            i = k + up * (3 - 2 * k)
            row = jnp.maximum(2 * up + i - off, 0)
            if k < 3:
                for c in range(3):
                    out[PA + k * 9 + c] = av[c, row]
                    out[PV + k * 3 + c] = fv[c, k + up]
                for c in range(6):
                    out[PA + k * 9 + 3 + c] = as_[c, row]
                    out[PS + k * 6 + c] = fs[c, i]
                out[PR + k] = rho[k + up]
            else:
                for j, c in enumerate(X3):
                    out[PA + 27 + j] = as_[c, row]
                    out[PS + 18 + j] = fs[c, 3 - up]
        for i in range(2):
            for c in range(2):
                out[PL + i * 2 + c] = lam[c, i]


def window_kernel(offsets, fv, fs, rho, lam, av, as_, ra, rb, w):
    odd, off, noff, _, _ = where_am_i(offsets)
    low_is_a = odd == 1

    def low(n):
        return jnp.where(low_is_a, ra[n], rb[n])

    def high(n):
        return jnp.where(low_is_a, rb[n], ra[n])

    def adjoint(p, ref, c, slot):
        k = 3 - p if p < 5 else p - 6
        n = PA + k * 9 + slot if k < 3 else PA + 27 + X3.index(c)
        if p < 2:
            return low(n)
        if p > 7:
            return high(n)
        j = p - 2
        own = ref[c, jnp.clip(j - off, 0, 5)]
        if j < 2:
            return jnp.where(j < off, low(n), own)
        if j > 3:
            return jnp.where(j - 4 < noff, own, high(n))
        return own

    for p in range(10):
        for c in range(6) if 1 <= p <= 8 else X3:
            if p == 0:
                f = low(PS + 18 + X3.index(c))
            elif p == 1:
                f = low(PS + c)
            elif p < 6:
                f = fs[c, p - 2]
            elif p < 9:
                f = high(PS + (p - 6) * 6 + c)
            else:
                f = high(PS + 18 + X3.index(c))
            w[entry_s(p, c)] = f
            w[entry_s(p, 6 + c)] = adjoint(p, as_, c, 3 + c)
    for p in range(1, 9):
        for c in range(3):
            if p < 2:
                f = low(PV + 2 * 3 + c)
            elif p < 6:
                f = fv[c, p - 2]
            else:
                f = high(PV + (p - 6) * 3 + c)
            w[VB + (p - 1) * 6 + c] = f
            w[VB + (p - 1) * 6 + 3 + c] = adjoint(p, av, c, c)
        if p < 2:
            r = low(PR + 2)
        elif p < 6:
            r = rho[p - 2]
        else:
            r = high(PR + p - 6)
        live = r > 0.0
        w[CB + p - 1] = jnp.where(live, (0.5 * H) / jnp.where(live, r, 1.0), 0.0)
    for p in range(2, 8):
        for c, base in ((0, LB), (1, MB)):
            m = lam[c, p - 2] if p < 6 else high(PL + (p - 6) * 2 + c)
            w[base + p - 2] = (0.5 * H) * m


def lanes():
    return lax.broadcasted_iota(jnp.int32, (8, 128), 1)


def y_tile(gy_odd, w, ga, gb, t, n):
    if t == 1:
        return w[n]
    return jnp.where((gy_odd == 1) == (t == 0), ga[n], gb[n])


def edge_kernel(offsets, w, ga, gb, out_a, out_b):
    _, _, _, gy_odd, gz_odd = where_am_i(offsets)
    lane = lanes()
    even = lax.rem(lane, 16) < 8

    def group(g, carry):
        for t in range(3):
            packed = []
            for half in range(2):
                acc = None
                for k in range(8):
                    x = y_tile(gy_odd, w, ga, gb, t, g * 16 + half * 8 + k)
                    x = pltpu.roll(x, (8 + 16 * k) % 128, 1)
                    acc = x if k == 0 else jnp.where(lane < 16 * k, acc, x)
                packed.append(acc)
            upper = jnp.where(even, packed[0], pltpu.roll(packed[1], 8, 1))
            lower = jnp.where(even, pltpu.roll(packed[0], 120, 1), packed[1])
            n = t * (N // 16) + g
            out_a[n] = jnp.where(gz_odd == 1, lower, upper)
            out_b[n] = jnp.where(gz_odd == 1, upper, lower)
        return carry

    lax.fori_loop(0, N // 16, group, 0)


def rows_diff(x):
    return pltpu.roll(x, 23, 0) - pltpu.roll(x, 1, 0)


def lanes_diff(x):
    return pltpu.roll(x, 255, 1) - pltpu.roll(x, 1, 1)


def cut(f):
    return f[8:16, 0:128]


def cut(f):
    return f[8:16, 0:128]


def velocity_step(planes, coef_at, stress_at, v_old, v_new, base):
    for p in planes:
        coef = coef_at(p)
        for q in range(2):
            for i in range(3):
                x, y, z = PAIRS[i]
                force = stress_at(p + 1, q * 6 + x) - stress_at(p - 1, q * 6 + x)
                force = force + rows_diff(stress_at(p, q * 6 + y))
                force = force + lanes_diff(stress_at(p, q * 6 + z))
                e = q * 3 + i
                step = coef * force
                old = v_old(p, e)
                v_new[(p - base) * 6 + e] = old - step if q == 0 else old + step


def stress_step(planes, lame_at, stress_at, v, v_base, kern_old, kern, s_new=None, s_base=2):
    last = s_new is None
    keep = cut if last else (lambda f: f)
    own_cut = (lambda f: f) if last else cut
    for p in planes:
        if not last:
            lam, mu = lame_at(p)
        traces, diags, shears, vels = [], [], [], []
        for q in range(2):
            n = (p - v_base) * 6 + q * 3
            own = [v[n + i] for i in range(3)]
            dx = [keep(v[n + 6 + i]) - keep(v[n - 6 + i]) for i in range(3)]
            dy = [keep(rows_diff(f)) for f in own]
            dz = [keep(lanes_diff(f)) for f in own]
            diag = [dx[0], dy[1], dz[2]]
            shear = [dy[2] + dz[1], dx[2] + dz[0], dx[1] + dy[0]]
            trace = diag[0] + diag[1] + diag[2]
            if not last:
                iso = lam * trace
                for c in range(3):
                    a = iso + (2.0 * mu) * diag[c]
                    b = mu * shear[c]
                    e = q * 6 + c
                    n = (p - s_base) * 12 + e
                    if q == 0:
                        s_new[n] = stress_at(p, e) - a
                        s_new[n + 3] = stress_at(p, e + 3) - b
                    else:
                        s_new[n] = stress_at(p, e) + a
                        s_new[n + 3] = stress_at(p, e + 3) + b
            if 2 <= p < 8:
                traces.append(own_cut(trace))
                diags.append([own_cut(f) for f in diag])
                shears.append([own_cut(f) for f in shear])
                vels.append([cut(f) for f in own])
        if not 2 <= p < 8:
            continue
        dot = lambda pair: (
            pair[0][0] * pair[1][0] + pair[0][1] * pair[1][1] + pair[0][2] * pair[1][2]
        )
        new = (
            H * dot(vels),
            (0.25 * H) * (traces[0] * traces[1]),
            (0.5 * H) * dot(diags) + (0.25 * H) * dot(shears),
        )
        for k in range(3):
            n = 6 * k + p - 2
            kern[n] = new[k] if kern_old is None else kern_old[n] + new[k]


def face_blocks(spec):
    blocks = [("own", [item]) for items, _ in spec for item in items]
    for items, m in spec:
        if m == 5:
            blocks += [(4, [item]) for item in items]
            blocks += [(5, items[k : k + 4]) for k in range(0, len(items), 4)]
        elif m:
            size = 4 // m
            blocks += [(m, items[k : k + size]) for k in range(0, len(items), size)]
    return blocks


def face_tiles(spec):
    count = len(face_blocks(spec))
    return count + -(-count // 8)


def face_places(spec):
    items = [item for group, _ in spec for item in group]
    return {item: k for k, item in enumerate(items)}, len(items)


def write_faces(odd, spec, st, s_new, v_new, face_a, face_b):
    lane = lanes()
    row = lax.broadcasted_iota(jnp.int32, (8, 256), 0)
    blocks = face_blocks(spec)
    count = len(blocks)
    for face, up in ((face_a, 1 - odd), (face_b, odd)):

        def source(item):
            kind, dx, e = item
            p = (3 + dx) + up * (3 - 2 * dx)
            if kind == "s":
                return s_new, (p - 2) * 12 + e
            if kind == "v":
                return v_new, (p - 1) * 6 + e
            return st, {"c": CB - 1, "l": LB - 2, "m": MB - 2}[kind] + p

        acc = None
        for j, (kind, items) in enumerate(blocks):
            if kind == "own":
                ref, n = source(items[0])
                x = ref[n, 8:16, :]
            else:
                m, x = kind, None
                for k, item in enumerate(items):
                    ref, n = source(item)
                    low, high = ref[n, 0:8, :], ref[n, 16:24, :]
                    if m == 5:
                        c = pltpu.roll(jnp.where(row == 3, low, high), (2 * k + 5) % 8, 0)
                        x = c if x is None else jnp.where(row < 2 * k, x, c)
                        continue
                    c = jnp.where(row < 4, high, low)
                    if m < 4:
                        c = pltpu.roll(c, (m + 2 * m * k) % 8, 0)
                    x = c if x is None else jnp.where(row < 2 * m * k, x, c)
            face[j] = x[:, 0:128]
            k = j % 8
            h = pltpu.roll(x[:, 128:256], (8 + 16 * k) % 128, 1)
            acc = h if k == 0 else jnp.where(lane < 16 * k, acc, h)
            if k == 7 or j == count - 1:
                face[count + j // 8] = acc


def read_faces(odd, spec, ra, rb, halo):
    lane = lanes()
    edge = (lane < 8) | (lane >= 120)
    low_is_a = odd == 1
    blocks = face_blocks(spec)
    count = len(blocks)
    place, total = face_places(spec)
    for low in (True, False):
        first = 0 if low else total
        pick = low_is_a if low else jnp.logical_not(low_is_a)
        get = lambda n: jnp.where(pick, ra[n], rb[n])
        packed = None
        for j, (kind, items) in enumerate(blocks):
            k = j % 8
            if k == 0:
                packed = get(count + j // 8)
            h = pltpu.roll(packed, (120 - 16 * k) % 128, 1)
            x = jnp.concatenate([get(j), jnp.where(edge, h, 0.0)], axis=1)
            for i, item in enumerate(items):
                n = first + place[item]
                if kind == "own":
                    halo[n, 8:16, :] = x
                elif kind == 5:
                    c = pltpu.roll(x, (11 - 2 * i) % 8, 0)
                    halo[n, 3:4, :] = c[3:4, :]
                    halo[n, 20:21, :] = c[4:5, :]
                else:
                    c = x if kind == 4 else pltpu.roll(x, (16 - kind - 2 * kind * i) % 8, 0)
                    halo[n, 0:8, :] = c
                    halo[n, 16:24, :] = c
        for items, m in spec:
            for item in items if m == 0 else ():
                halo[first + place[item], 0:8, :] = jnp.zeros((8, 256), jnp.float32)
                halo[first + place[item], 16:24, :] = jnp.zeros((8, 256), jnp.float32)


def first_kernel(offsets, w, ga, gb, za, zb, st, s_new, v_new, kern, face_a, face_b):
    odd, _, _, gy_odd, gz_odd = where_am_i(offsets)
    lane = lanes()

    even = lax.rem(lane, 16) < 8
    edge = (lane < 8) | (lane >= 120)

    def group(g, carry):
        for t in range(3):
            m = t * (N // 16) + g
            a, b = za[m], zb[m]
            low = jnp.where(gz_odd == 1, a, b)
            high = jnp.where(gz_odd == 1, b, a)
            packed = (
                jnp.where(even, low, pltpu.roll(high, 8, 1)),
                jnp.where(even, pltpu.roll(low, 120, 1), high),
            )
            for k in range(16):
                n = g * 16 + k
                st[n, 8 * t : 8 * t + 8, 0:128] = y_tile(gy_odd, w, ga, gb, t, n)
                x = pltpu.roll(packed[k // 8], (120 - 16 * (k % 8)) % 128, 1)
                st[n, 8 * t : 8 * t + 8, 128:256] = jnp.where(edge, x, 0.0)
        return carry

    lax.fori_loop(0, N // 16, group, 0)
    stress_at = lambda p, e: st[entry_s(p, e)]
    velocity_step(
        range(1, 9),
        lambda p: st[CB + p - 1],
        stress_at,
        lambda p, e: st[VB + (p - 1) * 6 + e],
        v_new,
        1,
    )
    lame_at = lambda p: (st[LB + p - 2], st[MB + p - 2])
    stress_step(range(2, 8), lame_at, stress_at, v_new, 1, None, kern, s_new)
    write_faces(odd, MID, st, s_new, v_new, face_a, face_b)


def reader(spec, halo):
    place, total = face_places(spec)

    def at(kind, p, first, e, inside):
        if first <= p <= 9 - first:
            return inside()
        low = p < first
        dx = 2 - p if low else p - 7
        return halo[place[(kind, dx, e)] + (0 if low else total)]

    return at


def middle_kernel(
    offsets, st, s_old, v_old, kern_old, ra, rb, s_new, v_new, kern, face_a, face_b, halo, s_mid, v_mid
):
    odd = where_am_i(offsets)[0]
    read_faces(odd, MID, ra, rb, halo)
    at = reader(MID, halo)
    coef_at = lambda p: at("c", p, 1, 0, lambda: st[CB + p - 1])
    lame_at = lambda p: (
        at("l", p, 2, 0, lambda: st[LB + p - 2]),
        at("m", p, 2, 0, lambda: st[MB + p - 2]),
    )
    stress_at = lambda p, e: at("s", p, 2, e, lambda: s_old[(p - 2) * 12 + e])
    v_at = lambda p, e: at("v", p, 1, e, lambda: v_old[(p - 1) * 6 + e])
    velocity_step(range(-1, 11), coef_at, stress_at, v_at, v_mid, -1)
    stress_step(range(0, 10), lame_at, stress_at, v_mid, -1, kern_old, kern, s_mid, 0)
    stress_mid = lambda p, e: s_mid[p * 12 + e]
    v_at_mid = lambda p, e: v_mid[(p + 1) * 6 + e]
    velocity_step(range(1, 9), coef_at, stress_mid, v_at_mid, v_new, 1)
    stress_step(range(2, 8), lame_at, stress_mid, v_new, 1, kern, kern, s_new)
    write_faces(odd, LAST, st, s_new, v_new, face_a, face_b)


def last_kernel(
    offsets, st, s_old, v_old, kern_old, ra, rb, dens, modu, halo, v_new, kern
):
    odd, off, noff, _, _ = where_am_i(offsets)
    read_faces(odd, LAST, ra, rb, halo)
    at = reader(LAST, halo)
    stress_at = lambda p, e: at("s", p, 2, e, lambda: s_old[(p - 2) * 12 + e])
    velocity_step(
        range(1, 9),
        lambda p: st[CB + p - 1],
        stress_at,
        lambda p, e: v_old[(p - 1) * 6 + e],
        v_new,
        1,
    )
    stress_step(range(2, 8), None, stress_at, v_new, 1, kern_old, kern)
    extent = 4 + noff - off
    for r in range(6):
        row = jnp.minimum(off + r, 5)
        live = r < extent
        dens[r] = jnp.where(live, kern[row], 0.0)
        modu[0, r] = jnp.where(live, kern[6 + row], 0.0)
        modu[1, r] = jnp.where(live, kern[12 + row], 0.0)


def call(kernel, name, outs, args, scratch=(), space=pltpu.VMEM):
    vmem = pl.BlockSpec(memory_space=pltpu.VMEM)
    return pl.pallas_call(
        kernel,
        out_shape=[jax.ShapeDtypeStruct(s, jnp.float32) for s in outs],
        in_specs=[pl.BlockSpec(memory_space=pltpu.SMEM)]
        + [pl.BlockSpec(memory_space=space)] * (len(args) - 1),
        out_specs=[vmem] * len(outs),
        scratch_shapes=[pltpu.VMEM(s, jnp.float32) if isinstance(s, tuple) else s for s in scratch],
        compiler_params=pltpu.CompilerParams(vmem_limit_bytes=VMEM_LIMIT),
        name=name,
    )(*args)


def shards(fwd_velocity, fwd_stress, density, lame, adj_velocity, adj_stress, offsets):
    raw = (fwd_velocity, fwd_stress, density, lame, adj_velocity, adj_stress)
    raw = [pltpu.with_memory_space_constraint(a, pltpu.HBM) for a in raw]
    send_a, send_b, *held = call(
        pack_kernel,
        "pack",
        [(NP1, 8, 128)] * 2 + [a.shape for a in raw],
        (offsets, *raw),
        [pltpu.SemaphoreType.DMA((6,))],
        pltpu.HBM,
    )
    recv = both_swaps(send_a, send_b, "grp")
    (win,) = call(window_kernel, "window", [(N, 8, 128)], (offsets, *held, *recv))
    ga, gb = both_swaps(win, win, "gy")
    edges = call(edge_kernel, "edge", [(3 * N // 16, 8, 128)] * 2, (offsets, win, ga, gb))
    za, zb = both_swaps(*edges, "gz")
    carried = [(72, 24, 256), (48, 24, 256), (18, 8, 128)]
    faces = lambda spec: [(face_tiles(spec), 8, 128)] * 2
    halos = lambda spec: (2 * face_places(spec)[1], 24, 256)
    state, *moving, face_a, face_b = call(
        first_kernel,
        "first",
        [(N, 24, 256)] + carried + faces(MID),
        (offsets, win, ga, gb, za, zb),
    )
    recv = both_swaps(face_a, face_b, "grp")
    *moving, face_a, face_b = call(
        middle_kernel,
        "middle",
        carried + faces(LAST),
        (offsets, state, *moving, *recv),
        [halos(MID), (120, 24, 256), (72, 24, 256)],
    )
    recv = both_swaps(face_a, face_b, "grp")
    dens, modu = call(
        last_kernel,
        "last",
        [(6, 8, 128), (2, 6, 8, 128)],
        (offsets, state, *moving, *recv),
        [halos(LAST), (48, 24, 256), (18, 8, 128)],
    )
    return dens, modu


def solution(mesh):
    return jax.shard_map(
        shards,
        mesh=mesh,
        in_specs=(
            P(None, "grp", "gy", "gz"),
            P(None, "grp", "gy", "gz"),
            P("grp", "gy", "gz"),
            P(None, "grp", "gy", "gz"),
            P(None, "grp", "gy", "gz"),
            P(None, "grp", "gy", "gz"),
            P(),
        ),
        out_specs=(P("grp", "gy", "gz"), P(None, "grp", "gy", "gz")),
        check_vma=False,
    )
```

```python
import jax
import jax.numpy as jnp
from jax import lax
from jax.experimental import pallas as pl
from jax.experimental.pallas import tpu as pltpu
from jax.sharding import PartitionSpec as P


H = 0.15
PAIRS = ((0, 5, 4), (5, 1, 3), (4, 3, 2))

EB, VB, CB, LB, MB, N = 96, 108, 156, 164, 170, 176
PA, PV, PS, PR, PL, NP1 = 0, 30, 39, 60, 63, 67
X3 = [0, 5, 4]
ALL12 = list(range(12))
X6 = [0, 5, 4, 6, 11, 10]


def entry_s(p, e):
    if 1 <= p <= 8:
        return (p - 1) * 12 + e
    return EB + (6 if p == 9 else 0) + X6.index(e)


MID = [
    ([("s", 1, e) for e in ALL12], 5),
    (
        [("s", dx, e) for dx in (2, 3) for e in ALL12]
        + [("v", 2, e) for e in range(6)]
        + [("c", 2, 0), ("l", 1, 0), ("m", 1, 0)],
        4,
    ),
    (
        [("s", 4, e) for e in X6]
        + [("v", 3, e) for e in range(6)]
        + [("c", 3, 0), ("l", 2, 0), ("m", 2, 0)],
        2,
    ),
]
LAST = [([("s", 1, e) for e in ALL12], 1), ([("s", 2, e) for e in X6], 0)]
VMEM_LIMIT = 16 << 20


def swaps(count, first):
    out = []
    for i in range(first, count - 1, 2):
        out += [(i, i + 1), (i + 1, i)]
    return out


def both_swaps(value_a, value_b, axis):
    count = lax.axis_size(axis)
    second = lax.ppermute(value_b, axis, swaps(count, 1))
    first = lax.ppermute(value_a, axis, swaps(count, 0))
    return first, second


def where_am_i(offsets):
    place = lax.axis_index("grp")
    last = lax.axis_size("grp") - 1
    off = offsets[place]
    noff = jnp.where(place < last, offsets[jnp.minimum(place + 1, last)], 0)
    return (
        lax.rem(place, 2),
        off,
        noff,
        lax.rem(lax.axis_index("gy"), 2),
        lax.rem(lax.axis_index("gz"), 2),
    )


def pack_kernel(offsets, *refs):
    raw, (out_a, out_b), held, sems = refs[:6], refs[6:8], refs[8:14], refs[14]
    copies = [pltpu.make_async_copy(raw[k], held[k], sems.at[k]) for k in range(6)]
    for copy in copies:
        copy.start()
    for copy in copies:
        copy.wait()
    fv, fs, rho, lam, av, as_ = held
    odd, off, _, _, _ = where_am_i(offsets)
    for out, up in ((out_a, 1 - odd), (out_b, odd)):
        for k in range(4):
            i = k + up * (3 - 2 * k)
            row = jnp.maximum(2 * up + i - off, 0)
            if k < 3:
                for c in range(3):
                    out[PA + k * 9 + c] = av[c, row]
                    out[PV + k * 3 + c] = fv[c, k + up]
                for c in range(6):
                    out[PA + k * 9 + 3 + c] = as_[c, row]
                    out[PS + k * 6 + c] = fs[c, i]
                out[PR + k] = rho[k + up]
            else:
                for j, c in enumerate(X3):
                    out[PA + 27 + j] = as_[c, row]
                    out[PS + 18 + j] = fs[c, 3 - up]
        for i in range(2):
            for c in range(2):
                out[PL + i * 2 + c] = lam[c, i]


def window_kernel(offsets, fv, fs, rho, lam, av, as_, ra, rb, w):
    odd, off, noff, _, _ = where_am_i(offsets)
    low_is_a = odd == 1

    def low(n):
        return jnp.where(low_is_a, ra[n], rb[n])

    def high(n):
        return jnp.where(low_is_a, rb[n], ra[n])

    def adjoint(p, ref, c, slot):
        k = 3 - p if p < 5 else p - 6
        n = PA + k * 9 + slot if k < 3 else PA + 27 + X3.index(c)
        if p < 2:
            return low(n)
        if p > 7:
            return high(n)
        j = p - 2
        own = ref[c, jnp.clip(j - off, 0, 5)]
        if j < 2:
            return jnp.where(j < off, low(n), own)
        if j > 3:
            return jnp.where(j - 4 < noff, own, high(n))
        return own

    for p in range(10):
        for c in range(6) if 1 <= p <= 8 else X3:
            if p == 0:
                f = low(PS + 18 + X3.index(c))
            elif p == 1:
                f = low(PS + c)
            elif p < 6:
                f = fs[c, p - 2]
            elif p < 9:
                f = high(PS + (p - 6) * 6 + c)
            else:
                f = high(PS + 18 + X3.index(c))
            w[entry_s(p, c)] = f
            w[entry_s(p, 6 + c)] = adjoint(p, as_, c, 3 + c)
    for p in range(1, 9):
        for c in range(3):
            if p < 2:
                f = low(PV + 2 * 3 + c)
            elif p < 6:
                f = fv[c, p - 2]
            else:
                f = high(PV + (p - 6) * 3 + c)
            w[VB + (p - 1) * 6 + c] = f
            w[VB + (p - 1) * 6 + 3 + c] = adjoint(p, av, c, c)
        if p < 2:
            r = low(PR + 2)
        elif p < 6:
            r = rho[p - 2]
        else:
            r = high(PR + p - 6)
        live = r > 0.0
        w[CB + p - 1] = jnp.where(live, (0.5 * H) / jnp.where(live, r, 1.0), 0.0)
    for p in range(2, 8):
        for c, base in ((0, LB), (1, MB)):
            m = lam[c, p - 2] if p < 6 else high(PL + (p - 6) * 2 + c)
            w[base + p - 2] = (0.5 * H) * m


def lanes():
    return lax.broadcasted_iota(jnp.int32, (8, 128), 1)


def y_tile(gy_odd, w, ga, gb, t, n):
    if t == 1:
        return w[n]
    return jnp.where((gy_odd == 1) == (t == 0), ga[n], gb[n])


def edge_kernel(offsets, w, ga, gb, out_a, out_b):
    _, _, _, gy_odd, gz_odd = where_am_i(offsets)
    lane = lanes()
    even = lax.rem(lane, 16) < 8

    def group(g):
        for t in range(3):
            packed = []
            for half in range(2):
                acc = None
                for k in range(8):
                    x = y_tile(gy_odd, w, ga, gb, t, g * 16 + half * 8 + k)
                    x = pltpu.roll(x, (8 + 16 * k) % 128, 1)
                    acc = x if k == 0 else jnp.where(lane < 16 * k, acc, x)
                packed.append(acc)
            upper = jnp.where(even, packed[0], pltpu.roll(packed[1], 8, 1))
            lower = jnp.where(even, pltpu.roll(packed[0], 120, 1), packed[1])
            n = t * (N // 16) + g
            out_a[n] = jnp.where(gz_odd == 1, lower, upper)
            out_b[n] = jnp.where(gz_odd == 1, upper, lower)

    for g in range(N // 16):
        group(g)


def rows_diff(x):
    return pltpu.roll(x, 23, 0) - pltpu.roll(x, 1, 0)


def lanes_diff(x):
    return pltpu.roll(x, 255, 1) - pltpu.roll(x, 1, 1)


def cut(f):
    return f[8:16, 0:128]


def cut(f):
    return f[8:16, 0:128]


def velocity_step(planes, coef_at, stress_at, v_old, v_new, base):
    for p in planes:
        coef = coef_at(p)
        for q in range(2):
            for i in range(3):
                x, y, z = PAIRS[i]
                force = stress_at(p + 1, q * 6 + x) - stress_at(p - 1, q * 6 + x)
                force = force + rows_diff(stress_at(p, q * 6 + y))
                force = force + lanes_diff(stress_at(p, q * 6 + z))
                e = q * 3 + i
                step = coef * force
                old = v_old(p, e)
                v_new[(p - base) * 6 + e] = old - step if q == 0 else old + step


def stress_step(planes, lame_at, stress_at, v, v_base, kern_old, kern, s_new=None, s_base=2):
    last = s_new is None
    keep = cut if last else (lambda f: f)
    own_cut = (lambda f: f) if last else cut
    for p in planes:
        if not last:
            lam, mu = lame_at(p)
        traces, diags, shears, vels = [], [], [], []
        for q in range(2):
            n = (p - v_base) * 6 + q * 3
            own = [v[n + i] for i in range(3)]
            dx = [keep(v[n + 6 + i]) - keep(v[n - 6 + i]) for i in range(3)]
            dy = [keep(rows_diff(f)) for f in own]
            dz = [keep(lanes_diff(f)) for f in own]
            diag = [dx[0], dy[1], dz[2]]
            shear = [dy[2] + dz[1], dx[2] + dz[0], dx[1] + dy[0]]
            trace = diag[0] + diag[1] + diag[2]
            if not last:
                iso = lam * trace
                for c in range(3):
                    a = iso + (2.0 * mu) * diag[c]
                    b = mu * shear[c]
                    e = q * 6 + c
                    n = (p - s_base) * 12 + e
                    if q == 0:
                        s_new[n] = stress_at(p, e) - a
                        s_new[n + 3] = stress_at(p, e + 3) - b
                    else:
                        s_new[n] = stress_at(p, e) + a
                        s_new[n + 3] = stress_at(p, e + 3) + b
            if 2 <= p < 8:
                traces.append(own_cut(trace))
                diags.append([own_cut(f) for f in diag])
                shears.append([own_cut(f) for f in shear])
                vels.append([cut(f) for f in own])
        if not 2 <= p < 8:
            continue
        dot = lambda pair: (
            pair[0][0] * pair[1][0] + pair[0][1] * pair[1][1] + pair[0][2] * pair[1][2]
        )
        new = (
            H * dot(vels),
            (0.25 * H) * (traces[0] * traces[1]),
            (0.5 * H) * dot(diags) + (0.25 * H) * dot(shears),
        )
        for k in range(3):
            n = 6 * k + p - 2
            kern[n] = new[k] if kern_old is None else kern_old[n] + new[k]


def face_blocks(spec):
    blocks = [("own", [item]) for items, _ in spec for item in items]
    for items, m in spec:
        if m == 5:
            blocks += [(4, [item]) for item in items]
            blocks += [(5, items[k : k + 4]) for k in range(0, len(items), 4)]
        elif m:
            size = 4 // m
            blocks += [(m, items[k : k + size]) for k in range(0, len(items), size)]
    return blocks


def face_tiles(spec):
    count = len(face_blocks(spec))
    return count + -(-count // 8)


def face_places(spec):
    items = [item for group, _ in spec for item in group]
    return {item: k for k, item in enumerate(items)}, len(items)


def write_faces(odd, spec, st, s_new, v_new, face_a, face_b):
    lane = lanes()
    row = lax.broadcasted_iota(jnp.int32, (8, 256), 0)
    blocks = face_blocks(spec)
    count = len(blocks)
    for face, up in ((face_a, 1 - odd), (face_b, odd)):

        def source(item):
            kind, dx, e = item
            p = (3 + dx) + up * (3 - 2 * dx)
            if kind == "s":
                return s_new, (p - 2) * 12 + e
            if kind == "v":
                return v_new, (p - 1) * 6 + e
            return st, {"c": CB - 1, "l": LB - 2, "m": MB - 2}[kind] + p

        acc = None
        for j, (kind, items) in enumerate(blocks):
            if kind == "own":
                ref, n = source(items[0])
                x = ref[n, 8:16, :]
            else:
                m, x = kind, None
                for k, item in enumerate(items):
                    ref, n = source(item)
                    low, high = ref[n, 0:8, :], ref[n, 16:24, :]
                    if m == 5:
                        c = pltpu.roll(jnp.where(row == 3, low, high), (2 * k + 5) % 8, 0)
                        x = c if x is None else jnp.where(row < 2 * k, x, c)
                        continue
                    c = jnp.where(row < 4, high, low)
                    if m < 4:
                        c = pltpu.roll(c, (m + 2 * m * k) % 8, 0)
                    x = c if x is None else jnp.where(row < 2 * m * k, x, c)
            face[j] = x[:, 0:128]
            k = j % 8
            h = pltpu.roll(x[:, 128:256], (8 + 16 * k) % 128, 1)
            acc = h if k == 0 else jnp.where(lane < 16 * k, acc, h)
            if k == 7 or j == count - 1:
                face[count + j // 8] = acc


def read_faces(odd, spec, ra, rb, halo):
    lane = lanes()
    edge = (lane < 8) | (lane >= 120)
    low_is_a = odd == 1
    blocks = face_blocks(spec)
    count = len(blocks)
    place, total = face_places(spec)
    for low in (True, False):
        first = 0 if low else total
        pick = low_is_a if low else jnp.logical_not(low_is_a)
        get = lambda n: jnp.where(pick, ra[n], rb[n])
        packed = None
        for j, (kind, items) in enumerate(blocks):
            k = j % 8
            if k == 0:
                packed = get(count + j // 8)
            h = pltpu.roll(packed, (120 - 16 * k) % 128, 1)
            x = jnp.concatenate([get(j), jnp.where(edge, h, 0.0)], axis=1)
            for i, item in enumerate(items):
                n = first + place[item]
                if kind == "own":
                    halo[n, 8:16, :] = x
                elif kind == 5:
                    c = pltpu.roll(x, (11 - 2 * i) % 8, 0)
                    halo[n, 3:4, :] = c[3:4, :]
                    halo[n, 20:21, :] = c[4:5, :]
                else:
                    c = x if kind == 4 else pltpu.roll(x, (16 - kind - 2 * kind * i) % 8, 0)
                    halo[n, 0:8, :] = c
                    halo[n, 16:24, :] = c
        for items, m in spec:
            for item in items if m == 0 else ():
                halo[first + place[item], 0:8, :] = jnp.zeros((8, 256), jnp.float32)
                halo[first + place[item], 16:24, :] = jnp.zeros((8, 256), jnp.float32)


def first_kernel(offsets, w, ga, gb, za, zb, st, s_new, v_new, kern, face_a, face_b):
    odd, _, _, gy_odd, gz_odd = where_am_i(offsets)
    lane = lanes()

    even = lax.rem(lane, 16) < 8
    edge = (lane < 8) | (lane >= 120)

    def group(g):
        for t in range(3):
            m = t * (N // 16) + g
            a, b = za[m], zb[m]
            low = jnp.where(gz_odd == 1, a, b)
            high = jnp.where(gz_odd == 1, b, a)
            packed = (
                jnp.where(even, low, pltpu.roll(high, 8, 1)),
                jnp.where(even, pltpu.roll(low, 120, 1), high),
            )
            for k in range(16):
                n = g * 16 + k
                st[n, 8 * t : 8 * t + 8, 0:128] = y_tile(gy_odd, w, ga, gb, t, n)
                x = pltpu.roll(packed[k // 8], (120 - 16 * (k % 8)) % 128, 1)
                st[n, 8 * t : 8 * t + 8, 128:256] = jnp.where(edge, x, 0.0)

    for g in range(N // 16):
        group(g)
    stress_at = lambda p, e: st[entry_s(p, e)]
    velocity_step(
        range(1, 9),
        lambda p: st[CB + p - 1],
        stress_at,
        lambda p, e: st[VB + (p - 1) * 6 + e],
        v_new,
        1,
    )
    lame_at = lambda p: (st[LB + p - 2], st[MB + p - 2])
    stress_step(range(2, 8), lame_at, stress_at, v_new, 1, None, kern, s_new)
    write_faces(odd, MID, st, s_new, v_new, face_a, face_b)


def reader(spec, halo):
    place, total = face_places(spec)

    def at(kind, p, first, e, inside):
        if first <= p <= 9 - first:
            return inside()
        low = p < first
        dx = 2 - p if low else p - 7
        return halo[place[(kind, dx, e)] + (0 if low else total)]

    return at


def middle_kernel(
    offsets, st, s_old, v_old, kern_old, ra, rb, s_new, v_new, kern, face_a, face_b, halo, s_mid, v_mid
):
    odd = where_am_i(offsets)[0]
    read_faces(odd, MID, ra, rb, halo)
    at = reader(MID, halo)
    coef_at = lambda p: at("c", p, 1, 0, lambda: st[CB + p - 1])
    lame_at = lambda p: (
        at("l", p, 2, 0, lambda: st[LB + p - 2]),
        at("m", p, 2, 0, lambda: st[MB + p - 2]),
    )
    stress_at = lambda p, e: at("s", p, 2, e, lambda: s_old[(p - 2) * 12 + e])
    v_at = lambda p, e: at("v", p, 1, e, lambda: v_old[(p - 1) * 6 + e])
    velocity_step(range(-1, 11), coef_at, stress_at, v_at, v_mid, -1)
    stress_step(range(0, 10), lame_at, stress_at, v_mid, -1, kern_old, kern, s_mid, 0)
    stress_mid = lambda p, e: s_mid[p * 12 + e]
    v_at_mid = lambda p, e: v_mid[(p + 1) * 6 + e]
    velocity_step(range(1, 9), coef_at, stress_mid, v_at_mid, v_new, 1)
    stress_step(range(2, 8), lame_at, stress_mid, v_new, 1, kern, kern, s_new)
    write_faces(odd, LAST, st, s_new, v_new, face_a, face_b)


def last_kernel(
    offsets, st, s_old, v_old, kern_old, ra, rb, dens, modu, halo, v_new, kern
):
    odd, off, noff, _, _ = where_am_i(offsets)
    read_faces(odd, LAST, ra, rb, halo)
    at = reader(LAST, halo)
    stress_at = lambda p, e: at("s", p, 2, e, lambda: s_old[(p - 2) * 12 + e])
    velocity_step(
        range(1, 9),
        lambda p: st[CB + p - 1],
        stress_at,
        lambda p, e: v_old[(p - 1) * 6 + e],
        v_new,
        1,
    )
    stress_step(range(2, 8), None, stress_at, v_new, 1, kern_old, kern)
    extent = 4 + noff - off
    for r in range(6):
        row = jnp.minimum(off + r, 5)
        live = r < extent
        dens[r] = jnp.where(live, kern[row], 0.0)
        modu[0, r] = jnp.where(live, kern[6 + row], 0.0)
        modu[1, r] = jnp.where(live, kern[12 + row], 0.0)


def call(kernel, outs, args, scratch=(), space=pltpu.VMEM):
    vmem = pl.BlockSpec(memory_space=pltpu.VMEM)
    return pl.pallas_call(
        kernel,
        out_shape=[jax.ShapeDtypeStruct(s, jnp.float32) for s in outs],
        in_specs=[pl.BlockSpec(memory_space=pltpu.SMEM)]
        + [pl.BlockSpec(memory_space=space)] * (len(args) - 1),
        out_specs=[vmem] * len(outs),
        scratch_shapes=[pltpu.VMEM(s, jnp.float32) if isinstance(s, tuple) else s for s in scratch],
        compiler_params=pltpu.CompilerParams(vmem_limit_bytes=VMEM_LIMIT),
    )(*args)


def sensitivity(fwd_velocity, fwd_stress, density, lame, adj_velocity, adj_stress, offsets):
    raw = (fwd_velocity, fwd_stress, density, lame, adj_velocity, adj_stress)
    raw = [pltpu.with_memory_space_constraint(a, pltpu.HBM) for a in raw]
    send_a, send_b, *held = call(
        pack_kernel,
        [(NP1, 8, 128)] * 2 + [a.shape for a in raw],
        (offsets, *raw),
        [pltpu.SemaphoreType.DMA((6,))],
        pltpu.HBM,
    )
    recv = both_swaps(send_a, send_b, "grp")
    (win,) = call(window_kernel, [(N, 8, 128)], (offsets, *held, *recv))
    ga, gb = both_swaps(win, win, "gy")
    edges = call(edge_kernel, [(3 * N // 16, 8, 128)] * 2, (offsets, win, ga, gb))
    za, zb = both_swaps(*edges, "gz")
    carried = [(72, 24, 256), (48, 24, 256), (18, 8, 128)]
    faces = lambda spec: [(face_tiles(spec), 8, 128)] * 2
    halos = lambda spec: (2 * face_places(spec)[1], 24, 256)
    state, *moving, face_a, face_b = call(
        first_kernel,
        [(N, 24, 256)] + carried + faces(MID),
        (offsets, win, ga, gb, za, zb),
    )
    recv = both_swaps(face_a, face_b, "grp")
    *moving, face_a, face_b = call(
        middle_kernel,
        carried + faces(LAST),
        (offsets, state, *moving, *recv),
        [halos(MID), (120, 24, 256), (72, 24, 256)],
    )
    recv = both_swaps(face_a, face_b, "grp")
    dens, modu = call(
        last_kernel,
        [(6, 8, 128), (2, 6, 8, 128)],
        (offsets, state, *moving, *recv),
        [halos(LAST), (48, 24, 256), (18, 8, 128)],
    )
    return dens, modu


def solution(mesh):
    return jax.shard_map(
        sensitivity,
        mesh=mesh,
        in_specs=(
            P(None, "grp", "gy", "gz"),
            P(None, "grp", "gy", "gz"),
            P("grp", "gy", "gz"),
            P(None, "grp", "gy", "gz"),
            P(None, "grp", "gy", "gz"),
            P(None, "grp", "gy", "gz"),
            P(),
        ),
        out_specs=(P("grp", "gy", "gz"), P(None, "grp", "gy", "gz")),
        check_vma=False,
    )
```

```python
import jax
import jax.numpy as jnp
from jax import lax
from jax.experimental import pallas as pl
from jax.experimental.pallas import tpu as pltpu
from jax.sharding import PartitionSpec as P


H = 0.15
PAIRS = ((0, 5, 4), (5, 1, 3), (4, 3, 2))

EB, VB, CB, LB, MB, N = 96, 108, 156, 164, 170, 176
PA, PV, PS, PR, PL, NP1 = 0, 30, 39, 60, 63, 67
X3 = [0, 5, 4]
ALL12 = list(range(12))
X6 = [0, 5, 4, 6, 11, 10]


def entry_s(p, e):
    if 1 <= p <= 8:
        return (p - 1) * 12 + e
    return EB + (6 if p == 9 else 0) + X6.index(e)


MID = [
    ([("s", 1, e) for e in ALL12], 5),
    (
        [("s", dx, e) for dx in (2, 3) for e in ALL12]
        + [("v", 2, e) for e in range(6)]
        + [("c", 2, 0), ("l", 1, 0), ("m", 1, 0)],
        4,
    ),
    (
        [("s", 4, e) for e in X6]
        + [("v", 3, e) for e in range(6)]
        + [("c", 3, 0), ("l", 2, 0), ("m", 2, 0)],
        2,
    ),
]
LAST = [([("s", 1, e) for e in ALL12], 1), ([("s", 2, e) for e in X6], 0)]
VMEM_LIMIT = 16 << 20


def swaps(count, first):
    out = []
    for i in range(first, count - 1, 2):
        out += [(i, i + 1), (i + 1, i)]
    return out


def both_swaps(value_a, value_b, axis):
    count = lax.axis_size(axis)
    second = lax.ppermute(value_b, axis, swaps(count, 1))
    first = lax.ppermute(value_a, axis, swaps(count, 0))
    return first, second


def where_am_i(offsets):
    place = lax.axis_index("grp")
    last = lax.axis_size("grp") - 1
    off = offsets[place]
    noff = jnp.where(place < last, offsets[jnp.minimum(place + 1, last)], 0)
    return (
        lax.rem(place, 2),
        off,
        noff,
        lax.rem(lax.axis_index("gy"), 2),
        lax.rem(lax.axis_index("gz"), 2),
    )


def pack_kernel(offsets, *refs):
    raw, (out_a, out_b), held, sems = refs[:6], refs[6:8], refs[8:14], refs[14]
    copies = [pltpu.make_async_copy(raw[k], held[k], sems.at[k]) for k in range(6)]
    for copy in copies:
        copy.start()
    for copy in copies:
        copy.wait()
    fv, fs, rho, lam, av, as_ = held
    odd, off, _, _, _ = where_am_i(offsets)
    for out, up in ((out_a, 1 - odd), (out_b, odd)):
        for k in range(4):
            i = k + up * (3 - 2 * k)
            row = jnp.maximum(2 * up + i - off, 0)
            if k < 3:
                for c in range(3):
                    out[PA + k * 9 + c] = av[c, row]
                    out[PV + k * 3 + c] = fv[c, k + up]
                for c in range(6):
                    out[PA + k * 9 + 3 + c] = as_[c, row]
                    out[PS + k * 6 + c] = fs[c, i]
                out[PR + k] = rho[k + up]
            else:
                for j, c in enumerate(X3):
                    out[PA + 27 + j] = as_[c, row]
                    out[PS + 18 + j] = fs[c, 3 - up]
        for i in range(2):
            for c in range(2):
                out[PL + i * 2 + c] = lam[c, i]


def window_kernel(offsets, fv, fs, rho, lam, av, as_, ra, rb, w):
    odd, off, noff, _, _ = where_am_i(offsets)
    low_is_a = odd == 1

    def low(n):
        return jnp.where(low_is_a, ra[n], rb[n])

    def high(n):
        return jnp.where(low_is_a, rb[n], ra[n])

    def adjoint(p, ref, c, slot):
        k = 3 - p if p < 5 else p - 6
        n = PA + k * 9 + slot if k < 3 else PA + 27 + X3.index(c)
        if p < 2:
            return low(n)
        if p > 7:
            return high(n)
        j = p - 2
        own = ref[c, jnp.clip(j - off, 0, 5)]
        if j < 2:
            return jnp.where(j < off, low(n), own)
        if j > 3:
            return jnp.where(j - 4 < noff, own, high(n))
        return own

    for p in range(10):
        for c in range(6) if 1 <= p <= 8 else X3:
            if p == 0:
                f = low(PS + 18 + X3.index(c))
            elif p == 1:
                f = low(PS + c)
            elif p < 6:
                f = fs[c, p - 2]
            elif p < 9:
                f = high(PS + (p - 6) * 6 + c)
            else:
                f = high(PS + 18 + X3.index(c))
            w[entry_s(p, c)] = f
            w[entry_s(p, 6 + c)] = adjoint(p, as_, c, 3 + c)
    for p in range(1, 9):
        for c in range(3):
            if p < 2:
                f = low(PV + 2 * 3 + c)
            elif p < 6:
                f = fv[c, p - 2]
            else:
                f = high(PV + (p - 6) * 3 + c)
            w[VB + (p - 1) * 6 + c] = f
            w[VB + (p - 1) * 6 + 3 + c] = adjoint(p, av, c, c)
        if p < 2:
            r = low(PR + 2)
        elif p < 6:
            r = rho[p - 2]
        else:
            r = high(PR + p - 6)
        live = r > 0.0
        w[CB + p - 1] = jnp.where(live, (0.5 * H) / jnp.where(live, r, 1.0), 0.0)
    for p in range(2, 8):
        for c, base in ((0, LB), (1, MB)):
            m = lam[c, p - 2] if p < 6 else high(PL + (p - 6) * 2 + c)
            w[base + p - 2] = (0.5 * H) * m


def lanes():
    return lax.broadcasted_iota(jnp.int32, (8, 128), 1)


def edge_kernel(offsets, *refs):
    tiles, (out_a, out_b) = refs[:-2], refs[-2:]
    _, _, _, _, gz_odd = where_am_i(offsets)
    lane = lanes()
    even = lax.rem(lane, 16) < 8

    def group(g, carry):
        for t, ref in enumerate(tiles):
            packed = []
            for half in range(2):
                acc = None
                for k in range(8):
                    x = pltpu.roll(ref[g * 16 + half * 8 + k], (8 + 16 * k) % 128, 1)
                    acc = x if k == 0 else jnp.where(lane < 16 * k, acc, x)
                packed.append(acc)
            upper = jnp.where(even, packed[0], pltpu.roll(packed[1], 8, 1))
            lower = jnp.where(even, pltpu.roll(packed[0], 120, 1), packed[1])
            n = t * (N // 16) + g
            out_a[n] = jnp.where(gz_odd == 1, lower, upper)
            out_b[n] = jnp.where(gz_odd == 1, upper, lower)
        return carry

    lax.fori_loop(0, N // 16, group, 0)


def rows_diff(x):
    return pltpu.roll(x, 23, 0) - pltpu.roll(x, 1, 0)


def lanes_diff(x):
    return pltpu.roll(x, 255, 1) - pltpu.roll(x, 1, 1)


def cut(f):
    return f[8:16, 0:128]


def cut(f):
    return f[8:16, 0:128]


def velocity_step(planes, coef_at, stress_at, v_old, v_new, base):
    for p in planes:
        coef = coef_at(p)
        for q in range(2):
            for i in range(3):
                x, y, z = PAIRS[i]
                force = stress_at(p + 1, q * 6 + x) - stress_at(p - 1, q * 6 + x)
                force = force + rows_diff(stress_at(p, q * 6 + y))
                force = force + lanes_diff(stress_at(p, q * 6 + z))
                e = q * 3 + i
                step = coef * force
                old = v_old(p, e)
                v_new[(p - base) * 6 + e] = old - step if q == 0 else old + step


def stress_step(planes, lame_at, stress_at, v, v_base, kern_old, kern, s_new=None, s_base=2):
    last = s_new is None
    keep = cut if last else (lambda f: f)
    own_cut = (lambda f: f) if last else cut
    for p in planes:
        if not last:
            lam, mu = lame_at(p)
        traces, diags, shears, vels = [], [], [], []
        for q in range(2):
            n = (p - v_base) * 6 + q * 3
            own = [v[n + i] for i in range(3)]
            dx = [keep(v[n + 6 + i]) - keep(v[n - 6 + i]) for i in range(3)]
            dy = [keep(rows_diff(f)) for f in own]
            dz = [keep(lanes_diff(f)) for f in own]
            diag = [dx[0], dy[1], dz[2]]
            shear = [dy[2] + dz[1], dx[2] + dz[0], dx[1] + dy[0]]
            trace = diag[0] + diag[1] + diag[2]
            if not last:
                iso = lam * trace
                for c in range(3):
                    a = iso + (2.0 * mu) * diag[c]
                    b = mu * shear[c]
                    e = q * 6 + c
                    n = (p - s_base) * 12 + e
                    if q == 0:
                        s_new[n] = stress_at(p, e) - a
                        s_new[n + 3] = stress_at(p, e + 3) - b
                    else:
                        s_new[n] = stress_at(p, e) + a
                        s_new[n + 3] = stress_at(p, e + 3) + b
            if 2 <= p < 8:
                traces.append(own_cut(trace))
                diags.append([own_cut(f) for f in diag])
                shears.append([own_cut(f) for f in shear])
                vels.append([cut(f) for f in own])
        if not 2 <= p < 8:
            continue
        dot = lambda pair: (
            pair[0][0] * pair[1][0] + pair[0][1] * pair[1][1] + pair[0][2] * pair[1][2]
        )
        new = (
            H * dot(vels),
            (0.25 * H) * (traces[0] * traces[1]),
            (0.5 * H) * dot(diags) + (0.25 * H) * dot(shears),
        )
        for k in range(3):
            n = 6 * k + p - 2
            kern[n] = new[k] if kern_old is None else kern_old[n] + new[k]


def face_blocks(spec):
    blocks = [("own", [item]) for items, _ in spec for item in items]
    for items, m in spec:
        if m == 5:
            blocks += [(4, [item]) for item in items]
            blocks += [(5, items[k : k + 4]) for k in range(0, len(items), 4)]
        elif m:
            size = 4 // m
            blocks += [(m, items[k : k + size]) for k in range(0, len(items), size)]
    return blocks


def face_tiles(spec):
    count = len(face_blocks(spec))
    return count + -(-count // 8)


def face_places(spec):
    items = [item for group, _ in spec for item in group]
    return {item: k for k, item in enumerate(items)}, len(items)


def write_faces(odd, spec, st, s_new, v_new, face_a, face_b):
    lane = lanes()
    row = lax.broadcasted_iota(jnp.int32, (8, 256), 0)
    blocks = face_blocks(spec)
    count = len(blocks)
    for face, up in ((face_a, 1 - odd), (face_b, odd)):

        def source(item):
            kind, dx, e = item
            p = (3 + dx) + up * (3 - 2 * dx)
            if kind == "s":
                return s_new, (p - 2) * 12 + e
            if kind == "v":
                return v_new, (p - 1) * 6 + e
            return st, {"c": CB - 1, "l": LB - 2, "m": MB - 2}[kind] + p

        acc = None
        for j, (kind, items) in enumerate(blocks):
            if kind == "own":
                ref, n = source(items[0])
                x = ref[n, 8:16, :]
            else:
                m, x = kind, None
                for k, item in enumerate(items):
                    ref, n = source(item)
                    low, high = ref[n, 0:8, :], ref[n, 16:24, :]
                    if m == 5:
                        c = pltpu.roll(jnp.where(row == 3, low, high), (2 * k + 5) % 8, 0)
                        x = c if x is None else jnp.where(row < 2 * k, x, c)
                        continue
                    c = jnp.where(row < 4, high, low)
                    if m < 4:
                        c = pltpu.roll(c, (m + 2 * m * k) % 8, 0)
                    x = c if x is None else jnp.where(row < 2 * m * k, x, c)
            face[j] = x[:, 0:128]
            k = j % 8
            h = pltpu.roll(x[:, 128:256], (8 + 16 * k) % 128, 1)
            acc = h if k == 0 else jnp.where(lane < 16 * k, acc, h)
            if k == 7 or j == count - 1:
                face[count + j // 8] = acc


def read_faces(odd, spec, ra, rb, halo):
    lane = lanes()
    edge = (lane < 8) | (lane >= 120)
    low_is_a = odd == 1
    blocks = face_blocks(spec)
    count = len(blocks)
    place, total = face_places(spec)
    for low in (True, False):
        first = 0 if low else total
        pick = low_is_a if low else jnp.logical_not(low_is_a)
        get = lambda n: jnp.where(pick, ra[n], rb[n])
        packed = None
        for j, (kind, items) in enumerate(blocks):
            k = j % 8
            if k == 0:
                packed = get(count + j // 8)
            h = pltpu.roll(packed, (120 - 16 * k) % 128, 1)
            x = jnp.concatenate([get(j), jnp.where(edge, h, 0.0)], axis=1)
            for i, item in enumerate(items):
                n = first + place[item]
                if kind == "own":
                    halo[n, 8:16, :] = x
                elif kind == 5:
                    c = pltpu.roll(x, (11 - 2 * i) % 8, 0)
                    halo[n, 3:4, :] = c[3:4, :]
                    halo[n, 20:21, :] = c[4:5, :]
                else:
                    c = x if kind == 4 else pltpu.roll(x, (16 - kind - 2 * kind * i) % 8, 0)
                    halo[n, 0:8, :] = c
                    halo[n, 16:24, :] = c
        for items, m in spec:
            for item in items if m == 0 else ():
                halo[first + place[item], 0:8, :] = jnp.zeros((8, 256), jnp.float32)
                halo[first + place[item], 16:24, :] = jnp.zeros((8, 256), jnp.float32)


def first_kernel(
    offsets, w, ga, gb, za, zb, fa, fb, st, s_new, v_new, kern, face_a, face_b
):
    odd, _, _, gy_odd, gz_odd = where_am_i(offsets)
    lane = lanes()
    even = lax.rem(lane, 16) < 8
    edge = (lane < 8) | (lane >= 120)

    def group(g, carry):
        for t in range(3):
            near = (gy_odd == 1) == (t == 0)
            if t == 1:
                a, b = za[g], zb[g]
            else:
                a = jnp.where(near, za[N // 16 + g], fa[g])
                b = jnp.where(near, zb[N // 16 + g], fb[g])
            low = jnp.where(gz_odd == 1, a, b)
            high = jnp.where(gz_odd == 1, b, a)
            packed = (
                jnp.where(even, low, pltpu.roll(high, 8, 1)),
                jnp.where(even, pltpu.roll(low, 120, 1), high),
            )
            for k in range(16):
                n = g * 16 + k
                x = w[n] if t == 1 else jnp.where(near, ga[n], gb[n])
                st[n, 8 * t : 8 * t + 8, 0:128] = x
                x = pltpu.roll(packed[k // 8], (120 - 16 * (k % 8)) % 128, 1)
                st[n, 8 * t : 8 * t + 8, 128:256] = jnp.where(edge, x, 0.0)
        return carry

    lax.fori_loop(0, N // 16, group, 0)
    stress_at = lambda p, e: st[entry_s(p, e)]
    velocity_step(
        range(1, 9),
        lambda p: st[CB + p - 1],
        stress_at,
        lambda p, e: st[VB + (p - 1) * 6 + e],
        v_new,
        1,
    )
    lame_at = lambda p: (st[LB + p - 2], st[MB + p - 2])
    stress_step(range(2, 8), lame_at, stress_at, v_new, 1, None, kern, s_new)
    write_faces(odd, MID, st, s_new, v_new, face_a, face_b)


def reader(spec, halo):
    place, total = face_places(spec)

    def at(kind, p, first, e, inside):
        if first <= p <= 9 - first:
            return inside()
        low = p < first
        dx = 2 - p if low else p - 7
        return halo[place[(kind, dx, e)] + (0 if low else total)]

    return at


def middle_kernel(
    offsets, st, s_old, v_old, kern_old, ra, rb, s_new, v_new, kern, face_a, face_b, halo, s_mid, v_mid
):
    odd = where_am_i(offsets)[0]
    read_faces(odd, MID, ra, rb, halo)
    at = reader(MID, halo)
    coef_at = lambda p: at("c", p, 1, 0, lambda: st[CB + p - 1])
    lame_at = lambda p: (
        at("l", p, 2, 0, lambda: st[LB + p - 2]),
        at("m", p, 2, 0, lambda: st[MB + p - 2]),
    )
    stress_at = lambda p, e: at("s", p, 2, e, lambda: s_old[(p - 2) * 12 + e])
    v_at = lambda p, e: at("v", p, 1, e, lambda: v_old[(p - 1) * 6 + e])
    velocity_step(range(-1, 11), coef_at, stress_at, v_at, v_mid, -1)
    stress_step(range(0, 10), lame_at, stress_at, v_mid, -1, kern_old, kern, s_mid, 0)
    stress_mid = lambda p, e: s_mid[p * 12 + e]
    v_at_mid = lambda p, e: v_mid[(p + 1) * 6 + e]
    velocity_step(range(1, 9), coef_at, stress_mid, v_at_mid, v_new, 1)
    stress_step(range(2, 8), lame_at, stress_mid, v_new, 1, kern, kern, s_new)
    write_faces(odd, LAST, st, s_new, v_new, face_a, face_b)


def last_kernel(
    offsets, st, s_old, v_old, kern_old, ra, rb, dens, modu, halo, v_new, kern
):
    odd, off, noff, _, _ = where_am_i(offsets)
    read_faces(odd, LAST, ra, rb, halo)
    at = reader(LAST, halo)
    stress_at = lambda p, e: at("s", p, 2, e, lambda: s_old[(p - 2) * 12 + e])
    velocity_step(
        range(1, 9),
        lambda p: st[CB + p - 1],
        stress_at,
        lambda p, e: v_old[(p - 1) * 6 + e],
        v_new,
        1,
    )
    stress_step(range(2, 8), None, stress_at, v_new, 1, kern_old, kern)
    extent = 4 + noff - off
    for r in range(6):
        row = jnp.minimum(off + r, 5)
        live = r < extent
        dens[r] = jnp.where(live, kern[row], 0.0)
        modu[0, r] = jnp.where(live, kern[6 + row], 0.0)
        modu[1, r] = jnp.where(live, kern[12 + row], 0.0)


def call(kernel, outs, args, scratch=(), space=pltpu.VMEM):
    vmem = pl.BlockSpec(memory_space=pltpu.VMEM)
    return pl.pallas_call(
        kernel,
        out_shape=[jax.ShapeDtypeStruct(s, jnp.float32) for s in outs],
        in_specs=[pl.BlockSpec(memory_space=pltpu.SMEM)]
        + [pl.BlockSpec(memory_space=space)] * (len(args) - 1),
        out_specs=[vmem] * len(outs),
        scratch_shapes=[pltpu.VMEM(s, jnp.float32) if isinstance(s, tuple) else s for s in scratch],
        compiler_params=pltpu.CompilerParams(vmem_limit_bytes=VMEM_LIMIT),
    )(*args)


def sensitivity(fwd_velocity, fwd_stress, density, lame, adj_velocity, adj_stress, offsets):
    raw = (fwd_velocity, fwd_stress, density, lame, adj_velocity, adj_stress)
    raw = [pltpu.with_memory_space_constraint(a, pltpu.HBM) for a in raw]
    send_a, send_b, *held = call(
        pack_kernel,
        [(NP1, 8, 128)] * 2 + [a.shape for a in raw],
        (offsets, *raw),
        [pltpu.SemaphoreType.DMA((6,))],
        pltpu.HBM,
    )
    recv = both_swaps(send_a, send_b, "grp")
    (win,) = call(window_kernel, [(N, 8, 128)], (offsets, *held, *recv))
    ga, gb = both_swaps(win, win, "gy")
    edges = call(edge_kernel, [(2 * N // 16, 8, 128)] * 2, (offsets, win, ga))
    za, zb = both_swaps(*edges, "gz")
    edges = call(edge_kernel, [(N // 16, 8, 128)] * 2, (offsets, gb))
    fa, fb = both_swaps(*edges, "gz")
    carried = [(72, 24, 256), (48, 24, 256), (18, 8, 128)]
    faces = lambda spec: [(face_tiles(spec), 8, 128)] * 2
    halos = lambda spec: (2 * face_places(spec)[1], 24, 256)
    state, *moving, face_a, face_b = call(
        first_kernel,
        [(N, 24, 256)] + carried + faces(MID),
        (offsets, win, ga, gb, za, zb, fa, fb),
    )
    recv = both_swaps(face_a, face_b, "grp")
    *moving, face_a, face_b = call(
        middle_kernel,
        carried + faces(LAST),
        (offsets, state, *moving, *recv),
        [halos(MID), (120, 24, 256), (72, 24, 256)],
    )
    recv = both_swaps(face_a, face_b, "grp")
    dens, modu = call(
        last_kernel,
        [(6, 8, 128), (2, 6, 8, 128)],
        (offsets, state, *moving, *recv),
        [halos(LAST), (48, 24, 256), (18, 8, 128)],
    )
    return dens, modu


def solution(mesh):
    return jax.shard_map(
        sensitivity,
        mesh=mesh,
        in_specs=(
            P(None, "grp", "gy", "gz"),
            P(None, "grp", "gy", "gz"),
            P("grp", "gy", "gz"),
            P(None, "grp", "gy", "gz"),
            P(None, "grp", "gy", "gz"),
            P(None, "grp", "gy", "gz"),
            P(),
        ),
        out_specs=(P("grp", "gy", "gz"), P(None, "grp", "gy", "gz")),
        check_vma=False,
    )
```

```python
import jax
import jax.numpy as jnp
from jax import lax
from jax.experimental import pallas as pl
from jax.experimental.pallas import tpu as pltpu
from jax.sharding import PartitionSpec as P


H = 0.15
PAIRS = ((0, 5, 4), (5, 1, 3), (4, 3, 2))

EB, VB, CB, LB, MB, N = 96, 108, 156, 164, 170, 176
PA, PV, PS, PR, PL, NP1 = 0, 30, 39, 60, 63, 67
X3 = [0, 5, 4]
ALL12 = list(range(12))
X6 = [0, 5, 4, 6, 11, 10]


def entry_s(p, e):
    if 1 <= p <= 8:
        return (p - 1) * 12 + e
    return EB + (6 if p == 9 else 0) + X6.index(e)


MID = [
    ([("s", 1, e) for e in ALL12], 5),
    (
        [("s", dx, e) for dx in (2, 3) for e in ALL12]
        + [("v", 2, e) for e in range(6)]
        + [("c", 2, 0), ("l", 1, 0), ("m", 1, 0)],
        4,
    ),
    (
        [("s", 4, e) for e in X6]
        + [("v", 3, e) for e in range(6)]
        + [("c", 3, 0), ("l", 2, 0), ("m", 2, 0)],
        2,
    ),
]
LAST = [([("s", 1, e) for e in ALL12], 1), ([("s", 2, e) for e in X6], 0)]
VMEM_LIMIT = 16 << 20


def swaps(count, first):
    out = []
    for i in range(first, count - 1, 2):
        out += [(i, i + 1), (i + 1, i)]
    return out


def both_swaps(value_a, value_b, axis):
    count = lax.axis_size(axis)
    second = lax.ppermute(value_b, axis, swaps(count, 1))
    first = lax.ppermute(value_a, axis, swaps(count, 0))
    return first, second


def where_am_i(offsets):
    place = lax.axis_index("grp")
    last = lax.axis_size("grp") - 1
    off = offsets[place]
    noff = jnp.where(place < last, offsets[jnp.minimum(place + 1, last)], 0)
    return (
        lax.rem(place, 2),
        off,
        noff,
        lax.rem(lax.axis_index("gy"), 2),
        lax.rem(lax.axis_index("gz"), 2),
    )


def pack_kernel(*refs):
    raw, (out_a, out_b), held, (offsets, sems) = refs[:7], refs[7:9], refs[9:15], refs[15:]
    to = (*held, offsets)
    copies = [pltpu.make_async_copy(raw[k], to[k], sems.at[k]) for k in range(7)]
    for copy in copies:
        copy.start()
    for copy in copies:
        copy.wait()
    fv, fs, rho, lam, av, as_ = held
    odd, off, _, _, _ = where_am_i(offsets)
    for out, up in ((out_a, 1 - odd), (out_b, odd)):
        for k in range(4):
            i = k + up * (3 - 2 * k)
            row = jnp.maximum(2 * up + i - off, 0)
            if k < 3:
                for c in range(3):
                    out[PA + k * 9 + c] = av[c, row]
                    out[PV + k * 3 + c] = fv[c, k + up]
                for c in range(6):
                    out[PA + k * 9 + 3 + c] = as_[c, row]
                    out[PS + k * 6 + c] = fs[c, i]
                out[PR + k] = rho[k + up]
            else:
                for j, c in enumerate(X3):
                    out[PA + 27 + j] = as_[c, row]
                    out[PS + 18 + j] = fs[c, 3 - up]
        for i in range(2):
            for c in range(2):
                out[PL + i * 2 + c] = lam[c, i]


def window_kernel(offsets, fv, fs, rho, lam, av, as_, ra, rb, w):
    odd, off, noff, _, _ = where_am_i(offsets)
    low_is_a = odd == 1

    def low(n):
        return jnp.where(low_is_a, ra[n], rb[n])

    def high(n):
        return jnp.where(low_is_a, rb[n], ra[n])

    def adjoint(p, ref, c, slot):
        k = 3 - p if p < 5 else p - 6
        n = PA + k * 9 + slot if k < 3 else PA + 27 + X3.index(c)
        if p < 2:
            return low(n)
        if p > 7:
            return high(n)
        j = p - 2
        own = ref[c, jnp.clip(j - off, 0, 5)]
        if j < 2:
            return jnp.where(j < off, low(n), own)
        if j > 3:
            return jnp.where(j - 4 < noff, own, high(n))
        return own

    for p in range(10):
        for c in range(6) if 1 <= p <= 8 else X3:
            if p == 0:
                f = low(PS + 18 + X3.index(c))
            elif p == 1:
                f = low(PS + c)
            elif p < 6:
                f = fs[c, p - 2]
            elif p < 9:
                f = high(PS + (p - 6) * 6 + c)
            else:
                f = high(PS + 18 + X3.index(c))
            w[entry_s(p, c)] = f
            w[entry_s(p, 6 + c)] = adjoint(p, as_, c, 3 + c)
    for p in range(1, 9):
        for c in range(3):
            if p < 2:
                f = low(PV + 2 * 3 + c)
            elif p < 6:
                f = fv[c, p - 2]
            else:
                f = high(PV + (p - 6) * 3 + c)
            w[VB + (p - 1) * 6 + c] = f
            w[VB + (p - 1) * 6 + 3 + c] = adjoint(p, av, c, c)
        if p < 2:
            r = low(PR + 2)
        elif p < 6:
            r = rho[p - 2]
        else:
            r = high(PR + p - 6)
        live = r > 0.0
        w[CB + p - 1] = jnp.where(live, (0.5 * H) / jnp.where(live, r, 1.0), 0.0)
    for p in range(2, 8):
        for c, base in ((0, LB), (1, MB)):
            m = lam[c, p - 2] if p < 6 else high(PL + (p - 6) * 2 + c)
            w[base + p - 2] = (0.5 * H) * m


def lanes():
    return lax.broadcasted_iota(jnp.int32, (8, 128), 1)


def in_pairs(group, count):
    def two(i, carry):
        group(2 * i)
        group(2 * i + 1)
        return carry

    lax.fori_loop(0, count // 2, two, 0)
    if count % 2:
        group(count - 1)


def y_tile(gy_odd, w, ga, gb, t, n):
    if t == 1:
        return w[n]
    return jnp.where((gy_odd == 1) == (t == 0), ga[n], gb[n])


def edge_kernel(offsets, w, ga, gb, out_a, out_b):
    _, _, _, gy_odd, gz_odd = where_am_i(offsets)
    lane = lanes()
    even = lax.rem(lane, 16) < 8

    def group(g):
        for t in range(3):
            packed = []
            for half in range(2):
                acc = None
                for k in range(8):
                    x = y_tile(gy_odd, w, ga, gb, t, g * 16 + half * 8 + k)
                    x = pltpu.roll(x, (8 + 16 * k) % 128, 1)
                    acc = x if k == 0 else jnp.where(lane < 16 * k, acc, x)
                packed.append(acc)
            upper = jnp.where(even, packed[0], pltpu.roll(packed[1], 8, 1))
            lower = jnp.where(even, pltpu.roll(packed[0], 120, 1), packed[1])
            n = t * (N // 16) + g
            out_a[n] = jnp.where(gz_odd == 1, lower, upper)
            out_b[n] = jnp.where(gz_odd == 1, upper, lower)

    in_pairs(group, N // 16)


def rows_diff(x):
    return pltpu.roll(x, 23, 0) - pltpu.roll(x, 1, 0)


def lanes_diff(x):
    return pltpu.roll(x, 255, 1) - pltpu.roll(x, 1, 1)


def cut(f):
    return f[8:16, 0:128]


def cut(f):
    return f[8:16, 0:128]


def velocity_step(planes, coef_at, stress_at, v_old, v_new, base):
    for p in planes:
        coef = coef_at(p)
        for q in range(2):
            for i in range(3):
                x, y, z = PAIRS[i]
                force = stress_at(p + 1, q * 6 + x) - stress_at(p - 1, q * 6 + x)
                force = force + rows_diff(stress_at(p, q * 6 + y))
                force = force + lanes_diff(stress_at(p, q * 6 + z))
                e = q * 3 + i
                step = coef * force
                old = v_old(p, e)
                v_new[(p - base) * 6 + e] = old - step if q == 0 else old + step


def stress_step(planes, lame_at, stress_at, v, v_base, kern_old, kern, s_new=None, s_base=2):
    last = s_new is None
    keep = cut if last else (lambda f: f)
    own_cut = (lambda f: f) if last else cut
    for p in planes:
        if not last:
            lam, mu = lame_at(p)
        traces, diags, shears, vels = [], [], [], []
        for q in range(2):
            n = (p - v_base) * 6 + q * 3
            own = [v[n + i] for i in range(3)]
            dx = [keep(v[n + 6 + i]) - keep(v[n - 6 + i]) for i in range(3)]
            dy = [keep(rows_diff(f)) for f in own]
            dz = [keep(lanes_diff(f)) for f in own]
            diag = [dx[0], dy[1], dz[2]]
            shear = [dy[2] + dz[1], dx[2] + dz[0], dx[1] + dy[0]]
            trace = diag[0] + diag[1] + diag[2]
            if not last:
                iso = lam * trace
                for c in range(3):
                    a = iso + (2.0 * mu) * diag[c]
                    b = mu * shear[c]
                    e = q * 6 + c
                    n = (p - s_base) * 12 + e
                    if q == 0:
                        s_new[n] = stress_at(p, e) - a
                        s_new[n + 3] = stress_at(p, e + 3) - b
                    else:
                        s_new[n] = stress_at(p, e) + a
                        s_new[n + 3] = stress_at(p, e + 3) + b
            if 2 <= p < 8:
                traces.append(own_cut(trace))
                diags.append([own_cut(f) for f in diag])
                shears.append([own_cut(f) for f in shear])
                vels.append([cut(f) for f in own])
        if not 2 <= p < 8:
            continue
        dot = lambda pair: (
            pair[0][0] * pair[1][0] + pair[0][1] * pair[1][1] + pair[0][2] * pair[1][2]
        )
        new = (
            H * dot(vels),
            (0.25 * H) * (traces[0] * traces[1]),
            (0.5 * H) * dot(diags) + (0.25 * H) * dot(shears),
        )
        for k in range(3):
            n = 6 * k + p - 2
            kern[n] = new[k] if kern_old is None else kern_old[n] + new[k]


def face_blocks(spec):
    blocks = [("own", [item]) for items, _ in spec for item in items]
    for items, m in spec:
        if m == 5:
            blocks += [(4, [item]) for item in items]
            blocks += [(5, items[k : k + 4]) for k in range(0, len(items), 4)]
        elif m:
            size = 4 // m
            blocks += [(m, items[k : k + size]) for k in range(0, len(items), size)]
    return blocks


def face_tiles(spec):
    count = len(face_blocks(spec))
    return count + -(-count // 8)


def face_places(spec):
    items = [item for group, _ in spec for item in group]
    return {item: k for k, item in enumerate(items)}, len(items)


def write_faces(odd, spec, st, s_new, v_new, face_a, face_b):
    lane = lanes()
    row = lax.broadcasted_iota(jnp.int32, (8, 256), 0)
    blocks = face_blocks(spec)
    count = len(blocks)
    for face, up in ((face_a, 1 - odd), (face_b, odd)):

        def source(item):
            kind, dx, e = item
            p = (3 + dx) + up * (3 - 2 * dx)
            if kind == "s":
                return s_new, (p - 2) * 12 + e
            if kind == "v":
                return v_new, (p - 1) * 6 + e
            return st, {"c": CB - 1, "l": LB - 2, "m": MB - 2}[kind] + p

        acc = None
        for j, (kind, items) in enumerate(blocks):
            if kind == "own":
                ref, n = source(items[0])
                x = ref[n, 8:16, :]
            else:
                m, x = kind, None
                for k, item in enumerate(items):
                    ref, n = source(item)
                    low, high = ref[n, 0:8, :], ref[n, 16:24, :]
                    if m == 5:
                        c = pltpu.roll(jnp.where(row == 3, low, high), (2 * k + 5) % 8, 0)
                        x = c if x is None else jnp.where(row < 2 * k, x, c)
                        continue
                    c = jnp.where(row < 4, high, low)
                    if m < 4:
                        c = pltpu.roll(c, (m + 2 * m * k) % 8, 0)
                    x = c if x is None else jnp.where(row < 2 * m * k, x, c)
            face[j] = x[:, 0:128]
            k = j % 8
            h = pltpu.roll(x[:, 128:256], (8 + 16 * k) % 128, 1)
            acc = h if k == 0 else jnp.where(lane < 16 * k, acc, h)
            if k == 7 or j == count - 1:
                face[count + j // 8] = acc


def read_faces(odd, spec, ra, rb, halo):
    lane = lanes()
    edge = (lane < 8) | (lane >= 120)
    low_is_a = odd == 1
    blocks = face_blocks(spec)
    count = len(blocks)
    place, total = face_places(spec)
    for low in (True, False):
        first = 0 if low else total
        pick = low_is_a if low else jnp.logical_not(low_is_a)
        get = lambda n: jnp.where(pick, ra[n], rb[n])
        packed = None
        for j, (kind, items) in enumerate(blocks):
            k = j % 8
            if k == 0:
                packed = get(count + j // 8)
            h = pltpu.roll(packed, (120 - 16 * k) % 128, 1)
            x = jnp.concatenate([get(j), jnp.where(edge, h, 0.0)], axis=1)
            for i, item in enumerate(items):
                n = first + place[item]
                if kind == "own":
                    halo[n, 8:16, :] = x
                elif kind == 5:
                    c = pltpu.roll(x, (11 - 2 * i) % 8, 0)
                    halo[n, 3:4, :] = c[3:4, :]
                    halo[n, 20:21, :] = c[4:5, :]
                else:
                    c = x if kind == 4 else pltpu.roll(x, (16 - kind - 2 * kind * i) % 8, 0)
                    halo[n, 0:8, :] = c
                    halo[n, 16:24, :] = c
        for items, m in spec:
            for item in items if m == 0 else ():
                halo[first + place[item], 0:8, :] = jnp.zeros((8, 256), jnp.float32)
                halo[first + place[item], 16:24, :] = jnp.zeros((8, 256), jnp.float32)


def first_kernel(offsets, w, ga, gb, za, zb, st, s_new, v_new, kern, face_a, face_b):
    odd, _, _, gy_odd, gz_odd = where_am_i(offsets)
    lane = lanes()

    even = lax.rem(lane, 16) < 8
    edge = (lane < 8) | (lane >= 120)

    def group(g):
        for t in range(3):
            m = t * (N // 16) + g
            a, b = za[m], zb[m]
            low = jnp.where(gz_odd == 1, a, b)
            high = jnp.where(gz_odd == 1, b, a)
            packed = (
                jnp.where(even, low, pltpu.roll(high, 8, 1)),
                jnp.where(even, pltpu.roll(low, 120, 1), high),
            )
            for k in range(16):
                n = g * 16 + k
                st[n, 8 * t : 8 * t + 8, 0:128] = y_tile(gy_odd, w, ga, gb, t, n)
                x = pltpu.roll(packed[k // 8], (120 - 16 * (k % 8)) % 128, 1)
                st[n, 8 * t : 8 * t + 8, 128:256] = jnp.where(edge, x, 0.0)

    in_pairs(group, N // 16)
    stress_at = lambda p, e: st[entry_s(p, e)]
    velocity_step(
        range(1, 9),
        lambda p: st[CB + p - 1],
        stress_at,
        lambda p, e: st[VB + (p - 1) * 6 + e],
        v_new,
        1,
    )
    lame_at = lambda p: (st[LB + p - 2], st[MB + p - 2])
    stress_step(range(2, 8), lame_at, stress_at, v_new, 1, None, kern, s_new)
    write_faces(odd, MID, st, s_new, v_new, face_a, face_b)


def reader(spec, halo):
    place, total = face_places(spec)

    def at(kind, p, first, e, inside):
        if first <= p <= 9 - first:
            return inside()
        low = p < first
        dx = 2 - p if low else p - 7
        return halo[place[(kind, dx, e)] + (0 if low else total)]

    return at


def middle_kernel(
    offsets, st, s_old, v_old, kern_old, ra, rb, s_new, v_new, kern, face_a, face_b, halo, s_mid, v_mid
):
    odd = where_am_i(offsets)[0]
    read_faces(odd, MID, ra, rb, halo)
    at = reader(MID, halo)
    coef_at = lambda p: at("c", p, 1, 0, lambda: st[CB + p - 1])
    lame_at = lambda p: (
        at("l", p, 2, 0, lambda: st[LB + p - 2]),
        at("m", p, 2, 0, lambda: st[MB + p - 2]),
    )
    stress_at = lambda p, e: at("s", p, 2, e, lambda: s_old[(p - 2) * 12 + e])
    v_at = lambda p, e: at("v", p, 1, e, lambda: v_old[(p - 1) * 6 + e])
    velocity_step(range(-1, 11), coef_at, stress_at, v_at, v_mid, -1)
    stress_step(range(0, 10), lame_at, stress_at, v_mid, -1, kern_old, kern, s_mid, 0)
    stress_mid = lambda p, e: s_mid[p * 12 + e]
    v_at_mid = lambda p, e: v_mid[(p + 1) * 6 + e]
    velocity_step(range(1, 9), coef_at, stress_mid, v_at_mid, v_new, 1)
    stress_step(range(2, 8), lame_at, stress_mid, v_new, 1, kern, kern, s_new)
    write_faces(odd, LAST, st, s_new, v_new, face_a, face_b)


def last_kernel(
    offsets, st, s_old, v_old, kern_old, ra, rb, dens, modu, halo, v_new, kern
):
    odd, off, noff, _, _ = where_am_i(offsets)
    read_faces(odd, LAST, ra, rb, halo)
    at = reader(LAST, halo)
    stress_at = lambda p, e: at("s", p, 2, e, lambda: s_old[(p - 2) * 12 + e])
    velocity_step(
        range(1, 9),
        lambda p: st[CB + p - 1],
        stress_at,
        lambda p, e: v_old[(p - 1) * 6 + e],
        v_new,
        1,
    )
    stress_step(range(2, 8), None, stress_at, v_new, 1, kern_old, kern)
    extent = 4 + noff - off
    for r in range(6):
        row = jnp.minimum(off + r, 5)
        live = r < extent
        dens[r] = jnp.where(live, kern[row], 0.0)
        modu[0, r] = jnp.where(live, kern[6 + row], 0.0)
        modu[1, r] = jnp.where(live, kern[12 + row], 0.0)


def call(kernel, outs, args, scratch=()):
    vmem = pl.BlockSpec(memory_space=pltpu.VMEM)
    return pl.pallas_call(
        kernel,
        out_shape=[jax.ShapeDtypeStruct(s, jnp.float32) for s in outs],
        in_specs=[pl.BlockSpec(memory_space=pltpu.SMEM)]
        + [vmem] * (len(args) - 1),
        out_specs=[vmem] * len(outs),
        scratch_shapes=[pltpu.VMEM(s, jnp.float32) for s in scratch],
        compiler_params=pltpu.CompilerParams(vmem_limit_bytes=VMEM_LIMIT),
    )(*args)


def sensitivity(fwd_velocity, fwd_stress, density, lame, adj_velocity, adj_stress, offsets):
    raw = (fwd_velocity, fwd_stress, density, lame, adj_velocity, adj_stress)
    hbm = pl.BlockSpec(memory_space=pltpu.HBM)
    send_a, send_b, *held = pl.pallas_call(
        pack_kernel,
        out_shape=[
            jax.ShapeDtypeStruct(s, jnp.float32)
            for s in [(NP1, 8, 128)] * 2 + [a.shape for a in raw]
        ],
        in_specs=[hbm] * 7,
        out_specs=[pl.BlockSpec(memory_space=pltpu.VMEM)] * 8,
        scratch_shapes=[pltpu.SMEM(offsets.shape, jnp.int32), pltpu.SemaphoreType.DMA((7,))],
        compiler_params=pltpu.CompilerParams(vmem_limit_bytes=VMEM_LIMIT),
        name="pack",
    )(*[pltpu.with_memory_space_constraint(a, pltpu.HBM) for a in (*raw, offsets)])
    recv = both_swaps(send_a, send_b, "grp")
    (win,) = call(window_kernel, [(N, 8, 128)], (offsets, *held, *recv))
    ga, gb = both_swaps(win, win, "gy")
    edges = call(edge_kernel, [(3 * N // 16, 8, 128)] * 2, (offsets, win, ga, gb))
    za, zb = both_swaps(*edges, "gz")
    carried = [(72, 24, 256), (48, 24, 256), (18, 8, 128)]
    faces = lambda spec: [(face_tiles(spec), 8, 128)] * 2
    halos = lambda spec: (2 * face_places(spec)[1], 24, 256)
    state, *moving, face_a, face_b = call(
        first_kernel,
        [(N, 24, 256)] + carried + faces(MID),
        (offsets, win, ga, gb, za, zb),
    )
    recv = both_swaps(face_a, face_b, "grp")
    *moving, face_a, face_b = call(
        middle_kernel,
        carried + faces(LAST),
        (offsets, state, *moving, *recv),
        [halos(MID), (120, 24, 256), (72, 24, 256)],
    )
    recv = both_swaps(face_a, face_b, "grp")
    dens, modu = call(
        last_kernel,
        [(6, 8, 128), (2, 6, 8, 128)],
        (offsets, state, *moving, *recv),
        [halos(LAST), (48, 24, 256), (18, 8, 128)],
    )
    return dens, modu


def solution(mesh):
    return jax.shard_map(
        sensitivity,
        mesh=mesh,
        in_specs=(
            P(None, "grp", "gy", "gz"),
            P(None, "grp", "gy", "gz"),
            P("grp", "gy", "gz"),
            P(None, "grp", "gy", "gz"),
            P(None, "grp", "gy", "gz"),
            P(None, "grp", "gy", "gz"),
            P(),
        ),
        out_specs=(P("grp", "gy", "gz"), P(None, "grp", "gy", "gz")),
        check_vma=False,
    )
```
